128 devices in a mesh: row: 8 (over z, core), col: 16 (over x, y).
Axes of the slice: x: 4, y: 4, z: 4, core: 2. Of those that a mesh axis runs over, the one named last changes fastest.
Arguments:
- normed: bfloat16 [8192, 7168], P(None, 'col'), may hold values from -44 to 44
- projection_weight: bfloat16 [7168, 3, 7168], P('col', None, 'row')
- adapter_down_weight: bfloat16 [7168, 16, 32], P(None, 'col'), may hold values from -0.0625 to 0.0625
- adapter_up_weight: bfloat16 [16, 2, 16, 7168], P(None, None, None, 'row'), may hold values from -0.47851562 to 0.47851562
- packed_prompt_length: int32 [64], replicated, may hold values from 64 to 512, as said below
- prompt_adapter_ids: int32 [64], replicated, may hold values from 0 to 63, as said below
- slot_adapter_ids: int32 [16], replicated, may hold values from 0 to 63, as said below
- prompt_page_slots: int32 [64, 4], replicated, may hold values from -1 to 159, as said below
Outputs:
- attended: bfloat16 [8192, 7168], P('col', 'row')
- kv_cache: bfloat16 [160, 128, 2, 7168], P('col', None, None, 'row')
The draws below stay inside these ranges and needn't reach their ends.
Inputs may be any that keep to these rules, and one draw needn't show every extreme that they name: `packed_prompt_length`: the 64 lengths sum to 8192; one of them is exactly 512 and one exactly 64. `slot_adapter_ids`: distinct adapter ids. `prompt_adapter_ids`: every entry is one of slot_adapter_ids, and every loaded adapter is named by at least one prompt. `prompt_page_slots`: entry [i, j] is -1 where 128 * j >= packed_prompt_length[i]; otherwise it lies among slots 10 * c to 10 * c + 9, where c is the block of 512 packed tokens that holds the page's last token. No slot is named twice.
All inputs are finite; a program needn't handle non-finite values.
Results may differ from the reference program's by a relative error of at most 0.0072.
Values may be sent and summed in bfloat16 or wider, within the bound.
A program may use at most 256 MiB of HBM per device.

```python
import jax
import jax.numpy as jnp
from jax import lax

MODEL_WIDTH = 7168
HEADS = 56
HEAD_DIM = 128
ADAPTER_RANK = 16
ADAPTERS = 64
LOADED_SLOTS = 16
TOK_DEV = 512
TOKENS = 8192
PAGE = 128
LMAX = 512
MINLEN = 64
MAXPAGES = 4
PROMPTS = 64
SLOTS_DEV = 10
PAGE_SLOTS = 160


def prompt_lengths(key):
    folded = jax.random.fold_in(key, 11)
    key_order, key_share = jax.random.split(folded, 2)
    shuffled = jax.random.permutation(key_order, PROMPTS)
    long_prompt = shuffled[0]
    short_prompt = shuffled[1]
    prompt_ids = jnp.arange(PROMPTS, dtype=jnp.int32)
    others = (prompt_ids != long_prompt) & (prompt_ids != short_prompt)
    shares = jnp.where(others, jax.random.randint(key_share, (PROMPTS,), 50, 101), 0).astype(jnp.int32)
    spare_rows = TOKENS - MINLEN * PROMPTS - (LMAX - MINLEN)
    extras = spare_rows * shares // jnp.sum(shares)
    leftover = spare_rows - jnp.sum(extras)
    ranked = jnp.cumsum(others.astype(jnp.int32)) - 1
    extras = extras + jnp.where(others & (ranked < leftover), 1, 0)
    lengths = MINLEN + extras + jnp.where(prompt_ids == long_prompt, LMAX - MINLEN, 0)
    return lengths.astype(jnp.int32)


def adapter_choice(key):
    folded = jax.random.fold_in(key, 23)
    key_one, key_two, key_three, key_four, key_five = jax.random.split(folded, 5)
    middle = (jax.random.permutation(key_one, ADAPTERS - 2) + 1).astype(jnp.int32)
    chosen = jnp.concatenate([jnp.array([0, ADAPTERS - 1], dtype=jnp.int32), middle[:LOADED_SLOTS - 2]])
    loaded = chosen[jax.random.permutation(key_two, LOADED_SLOTS)]
    shuffled = jax.random.permutation(key_three, PROMPTS)
    ranked = jnp.argsort(shuffled).astype(jnp.int32)
    first_pick = jax.random.randint(key_four, (PROMPTS,), 0, LOADED_SLOTS)
    second_pick = jax.random.randint(key_five, (PROMPTS,), 0, LOADED_SLOTS)
    skewed = first_pick * second_pick // LOADED_SLOTS
    slot_pick = jnp.where(ranked < LOADED_SLOTS, ranked, skewed).astype(jnp.int32)
    return (loaded.astype(jnp.int32), loaded[slot_pick].astype(jnp.int32))


def draw_packed_prompt_length(key, part):
    return prompt_lengths(key)


def draw_slot_adapter_ids(key, part):
    loaded, requested = adapter_choice(key)
    return loaded


def draw_prompt_adapter_ids(key, part):
    loaded, requested = adapter_choice(key)
    return requested


def draw_prompt_page_slots(key, part):
    lengths = prompt_lengths(key)
    prompt_ends = jnp.cumsum(lengths).astype(jnp.int32)
    first_tok = prompt_ends - lengths
    page_ids = jnp.arange(MAXPAGES, dtype=jnp.int32)
    live_page = PAGE * page_ids[None, :] < lengths[:, None]
    last_tok = first_tok[:, None] + jnp.minimum(lengths[:, None], PAGE * (page_ids[None, :] + 1)) - 1
    owner_col = last_tok // TOK_DEV
    flat_live = live_page.reshape(-1)
    flat_last = last_tok.reshape(-1)
    flat_owner = owner_col.reshape(-1)
    before = (flat_owner[None, :] == flat_owner[:, None]) & flat_live[None, :] & (flat_last[None, :] < flat_last[:, None])
    ranked = jnp.sum(before.astype(jnp.int32), axis=1)
    owners = PAGE_SLOTS // SLOTS_DEV
    scores = jax.random.randint(jax.random.fold_in(key, 31), (owners, SLOTS_DEV), 0, 65536) * SLOTS_DEV
    scores = scores + jnp.arange(SLOTS_DEV, dtype=jnp.int32)[None, :]
    orders = jnp.argsort(scores, axis=1).astype(jnp.int32)
    owner_safe = jnp.clip(flat_owner, 0, owners - 1)
    local_slot = orders[owner_safe, jnp.clip(ranked, 0, SLOTS_DEV - 1)]
    slot_table = jnp.where(flat_live, owner_safe * SLOTS_DEV + local_slot, -1)
    return slot_table.reshape(PROMPTS, MAXPAGES).astype(jnp.int32)


def draw_normed(key, part):
    key_base = jax.random.fold_in(jax.random.fold_in(key, 5), 0)
    drawn_rows = jnp.clip(jax.random.normal(key_base, (TOKENS, MODEL_WIDTH), jnp.float32), -4.0, 4.0)
    return drawn_rows.astype(jnp.bfloat16)


def draw_projection_weight(key, part):
    key_raw = jax.random.fold_in(jax.random.fold_in(key, 7), 0)
    raw_normal = jax.random.normal(key_raw, (MODEL_WIDTH, 3, MODEL_WIDTH), jnp.float32)
    return (raw_normal * MODEL_WIDTH ** (-0.5)).astype(jnp.bfloat16)


def steps_of(rng, dims, cuts, smallest, top_value):
    def one(axis_at, parts):
        heights = jax.random.uniform(jax.random.fold_in(jax.random.fold_in(rng, 6), axis_at), (parts,), jnp.float32, smallest / len(cuts), top_value / len(cuts))
        return jnp.repeat(jnp.exp(heights), dims[axis_at] // parts).reshape((-1,) + (1,) * (len(dims) - axis_at - 1))

    factor_of = one(*cuts[0])
    for cut in cuts[1:]:
        factor_of = factor_of * one(*cut)
    return factor_of


def scatter_about(stream_key, dims, width, limit, cuts=(), kind=jnp.bfloat16):
    values = jax.random.normal(stream_key, dims, jnp.float32) * width
    if len(cuts) > 0:
        values = steps_of(stream_key, dims, cuts, -0.22, 0.18) * values
    return jnp.clip(values, min=-limit, max=limit).astype(kind)


def setup_inputs(seed: int = 0) -> dict:
    key_of = jax.random.split(jax.random.key(seed), 9)
    normed = draw_normed(jax.random.fold_in(key_of[8], 71), 0)
    projection_weight = draw_projection_weight(jax.random.fold_in(key_of[8], 71), 0)
    adapter_down_weight = scatter_about(key_of[2], (MODEL_WIDTH, LOADED_SLOTS, 2 * ADAPTER_RANK), MODEL_WIDTH ** -0.5, 0.0625, ((1, 16),))
    adapter_up_weight = scatter_about(key_of[3], (LOADED_SLOTS, 2, ADAPTER_RANK, MODEL_WIDTH), 0.08, 0.47851562, ((3, 8),))
    packed_prompt_length = draw_packed_prompt_length(jax.random.fold_in(key_of[8], 71), 0)
    prompt_adapter_ids = draw_prompt_adapter_ids(jax.random.fold_in(key_of[8], 71), 0)
    slot_adapter_ids = draw_slot_adapter_ids(jax.random.fold_in(key_of[8], 71), 0)
    prompt_page_slots = draw_prompt_page_slots(jax.random.fold_in(key_of[8], 71), 0)
    return dict(normed=normed, projection_weight=projection_weight, adapter_down_weight=adapter_down_weight, adapter_up_weight=adapter_up_weight, packed_prompt_length=packed_prompt_length, prompt_adapter_ids=prompt_adapter_ids, slot_adapter_ids=slot_adapter_ids, prompt_page_slots=prompt_page_slots)


adapter_scale = 2.0
masked_score = -1e30


def reference(normed, projection_weight, adapter_down_weight, adapter_up_weight, packed_prompt_length, prompt_adapter_ids, slot_adapter_ids, prompt_page_slots):
    prompt_ends = jnp.cumsum(packed_prompt_length).astype(jnp.int32)
    prompt_starts = (prompt_ends - packed_prompt_length).astype(jnp.int32)
    positions = jnp.arange(TOKENS, dtype=jnp.int32)
    prompts = (jnp.sum((positions[:, None] >= prompt_starts[None, :]).astype(jnp.int32), axis=1) - 1).astype(jnp.int32)
    matched = slot_adapter_ids[None, :] == prompt_adapter_ids[:, None]
    slot_of = jnp.sum(jnp.where(matched, jnp.arange(LOADED_SLOTS, dtype=jnp.int32)[None, :], 0), axis=1).astype(jnp.int32)
    token_slots = slot_of[prompts]
    pick_slot = token_slots[:, None] == jnp.arange(LOADED_SLOTS, dtype=jnp.int32)[None, :]
    base_projection_sums = jnp.dot(normed, projection_weight.reshape(MODEL_WIDTH, 3 * MODEL_WIDTH), preferred_element_type=jnp.float32)
    combined_output = jnp.dot(normed, adapter_down_weight.reshape(MODEL_WIDTH, LOADED_SLOTS * 2 * ADAPTER_RANK), preferred_element_type=jnp.float32)
    combined_output = combined_output.reshape(TOKENS, LOADED_SLOTS, 2 * ADAPTER_RANK)
    down_projected_rows = jnp.sum(jnp.where(pick_slot[:, :, None], combined_output, 0.0), axis=1).astype(jnp.bfloat16)
    pick_half = pick_slot.astype(jnp.bfloat16)

    def reduced_rank_rows(low_part, slot_membership):
        token_spread = (pick_half[:, :, None] * low_part[:, None, :]).reshape(TOKENS, LOADED_SLOTS * ADAPTER_RANK)
        return jnp.dot(token_spread, adapter_up_weight[:, slot_membership].reshape(LOADED_SLOTS * ADAPTER_RANK, MODEL_WIDTH), preferred_element_type=jnp.float32)

    query_token_rows = (base_projection_sums[:, :MODEL_WIDTH] + adapter_scale * reduced_rank_rows(down_projected_rows[:, :ADAPTER_RANK], 0)).astype(jnp.bfloat16)
    key_rows = base_projection_sums[:, MODEL_WIDTH:2 * MODEL_WIDTH].astype(jnp.bfloat16)
    value_token_rows = (base_projection_sums[:, 2 * MODEL_WIDTH:] + adapter_scale * reduced_rank_rows(down_projected_rows[:, ADAPTER_RANK:], 1)).astype(jnp.bfloat16)
    allowed = (prompts[:, None] == prompts[None, :]) & (positions[None, :] <= positions[:, None])
    score_scale = HEAD_DIM ** -0.5

    def one_head(head_index):
        first_col = (head_index * HEAD_DIM).astype(jnp.int32)
        query_head = lax.dynamic_slice_in_dim(query_token_rows, first_col, HEAD_DIM, 1)
        key_head = lax.dynamic_slice_in_dim(key_rows, first_col, HEAD_DIM, 1)
        value_head = lax.dynamic_slice_in_dim(value_token_rows, first_col, HEAD_DIM, 1)
        scores = jnp.dot(query_head, key_head.T, preferred_element_type=jnp.float32) * score_scale
        peak_score = jnp.max(jnp.where(allowed, scores, masked_score), axis=1, keepdims=True)
        weight = jnp.where(allowed, jnp.exp(scores - peak_score), 0.0)
        denominator = jnp.sum(weight, axis=1, keepdims=True)
        summed = jnp.dot(weight.astype(jnp.bfloat16), value_head, preferred_element_type=jnp.float32)
        return (summed / denominator).astype(jnp.bfloat16)

    heads_out = lax.map(one_head, jnp.arange(HEADS, dtype=jnp.int32))
    attended = jnp.transpose(heads_out, (1, 0, 2)).reshape(TOKENS, MODEL_WIDTH)
    both_rows = jnp.stack([key_rows, value_token_rows], axis=1)
    page_ids = jnp.arange(MAXPAGES, dtype=jnp.int32)
    page_first = prompt_starts[:, None] + PAGE * page_ids[None, :]
    rows_used = jnp.clip(packed_prompt_length[:, None] - PAGE * page_ids[None, :], 0, PAGE)
    page_lines = jnp.arange(PAGE, dtype=jnp.int32)
    token_index = jnp.clip(page_first[:, :, None] + page_lines[None, None, :], 0, TOKENS - 1).astype(jnp.int32)
    live_rows = page_lines[None, None, :] < rows_used[:, :, None]
    page_data = jnp.where(live_rows[:, :, :, None, None], both_rows[token_index], jnp.zeros((), both_rows.dtype))
    destination = jnp.where(prompt_page_slots >= 0, prompt_page_slots, PAGE_SLOTS).reshape(-1).astype(jnp.int32)
    cache_pages = jnp.zeros((PAGE_SLOTS, PAGE, 2, MODEL_WIDTH), both_rows.dtype)
    cache_pages = cache_pages.at[destination].set(page_data.reshape(PROMPTS * MAXPAGES, PAGE, 2, MODEL_WIDTH), mode="drop")
    return attended, cache_pages
```

```python
import jax
import jax.numpy as jnp
from jax import lax
from jax.experimental import pallas as pl
from jax.experimental.pallas import tpu as pltpu
from jax.sharding import PartitionSpec as P

HEAD_DIM = 128
PAGE = 128
SLOTS_DEV = 10
HEADS_DEV = 7
SLOTS = 16
RANK = 16
TOK = 512
WID = 448
KEEP = 640
BAND = 640

adapter_scale = 2.0
masked_score = -1e30
MESH = pl.DeviceIdType.MESH


def place():
    col = lax.axis_index("col")
    row = lax.axis_index("row")
    x, y = col // 4, col % 4
    z, k = row // 2, row % 2
    p = y // 2
    d = (k + p) % 2
    tok = x * 4 + y + d * (3 - 2 * y)
    return x, y, z, k, p, d, tok


def dev(x, y, z, k):
    return (z * 2 + k, x * 4 + y)


def fused(
    nt_ref,
    w_ref,
    at_ref,
    up_ref,
    tslot_ref,
    lo_ref,
    out_att,
    out_k,
    out_v,
    wbuf,
    nbuf,
    abuf,
    ubuf,
    raw,
    stage,
    kvwin,
    qbuf,
    att,
    acc,
    dpart,
    drecv,
    spread,
    rs,
    ss,
    ns,
    nss,
    as_,
    ass,
    ds_,
    dss,
    us,
    uss,
    raws,
    os_,
    oss,
):
    x, y, z, k, p, d, tok = place()
    xp, xm, xf = (x + 1) % 4, (x + 3) % 4, (x + 2) % 4
    zp, zm, zf = (z + 1) % 4, (z + 3) % 4, (z + 2) % 4
    mate = y + 1 - 2 * (y % 2)
    d_xp = dev(xp, y, z, k)
    d_xm = dev(xm, y, z, k)
    d_m = dev(x, mate, z, k)
    d_core = dev(x, y, z, 1 - k)
    d_swap = dev(x, 3 - y, z, 1 - k)
    d_cross = dev(x, 3 - y, z, k)
    d_zp = dev(x, y, zp, k)
    d_zm = dev(x, y, zm, k)
    b_own = (y + d) % 2
    q_own = 2 * d + b_own
    q_mate = 2 * d + 1 - b_own
    o_own = 2 * (1 - d) + (y + 1 - d) % 2
    o_mate = 2 * (1 - d) + 1 - (y + 1 - d) % 2
    lane0 = d == 0
    lane1 = d == 1
    b_src = y % 2
    xz = (x + z) % 4

    def rc(src, dst, send, recv, to):
        return pltpu.make_async_remote_copy(
            src_ref=src, dst_ref=dst, send_sem=send, recv_sem=recv, device_id=to, device_id_type=MESH
        )

    def got(ref, sem):
        rc(ref, ref, ss.at[0], sem, d_core).wait_recv()

    def sent(ref, sem):
        rc(ref, ref, sem, rs.at[0, 0], d_core).wait_send()

    def w_own(h):
        for j in range(3):
            src = w_ref.at[j, :, pl.ds(pl.multiple_of(h * HEAD_DIM, HEAD_DIM), HEAD_DIM)]
            lanes = pl.ds(j * HEAD_DIM, HEAD_DIM)

            @pl.when(lane0)
            def _():
                pltpu.make_async_copy(src, wbuf.at[h, q_own, x, :, lanes], rs.at[10, h]).start()

            @pl.when(lane1)
            def _():
                rc(src, wbuf.at[h, 2 + b_src, x, :, lanes], ss.at[10], rs.at[10, h], d_swap).start()

    for j in range(2):
        yt = y if j == 0 else mate
        xt = (x + 4 - z) % 4
        tt = xt * 4 + yt + d * (3 - 2 * yt)
        pltpu.make_async_copy(
            nt_ref.at[:, pl.ds(pl.multiple_of(tt * TOK, TOK), TOK)], raw.at[j], raws.at[j]
        ).start()
    w_own(0)
    w_own(1)

    @pl.when(tok == 0)
    def _():
        kvwin[:, 0:TOK, :] = jnp.zeros((HEADS_DEV, TOK, 2 * HEAD_DIM), jnp.bfloat16)

    for j in range(2):
        yt = y if j == 0 else mate
        xt = (x + 4 - z) % 4
        tt = xt * 4 + yt + d * (3 - 2 * yt)
        pltpu.make_async_copy(
            nt_ref.at[:, pl.ds(pl.multiple_of(tt * TOK, TOK), TOK)], raw.at[j], raws.at[j]
        ).wait()
        stage[j] = raw[j].T
        if j == 0:

            @pl.when(z == 0)
            def _():
                pltpu.make_async_copy(stage.at[0], nbuf.at[b_src, x], ns.at[b_src]).start()
                pltpu.make_async_copy(at_ref, abuf.at[b_src], as_.at[b_src]).start()

            @pl.when(z != 0)
            def _():
                rc(stage.at[0], nbuf.at[b_src, x], nss.at[0], ns.at[b_src], dev(xt, y, z, k)).start()
                rc(at_ref, abuf.at[b_src], ass.at[0], as_.at[b_src], dev(xt, y, z, k)).start()
        else:
            rc(stage.at[1], nbuf.at[b_src, x], nss.at[1], ns.at[b_src], dev(xt, mate, z, k)).start()
            rc(at_ref, abuf.at[b_src], ass.at[1], as_.at[b_src], dev(xt, mate, z, k)).start()

    @pl.when(lane0)
    def _():
        pltpu.make_async_copy(up_ref, ubuf, us).start()
        rc(up_ref, ubuf, uss, us, d_core).start()

    def down():
        for j in range(2):
            total = jnp.zeros((TOK, 2 * RANK), jnp.float32)
            for q in range(4):
                for xx in range(4):
                    first = (xx * 2 + (p + q // 2) % 2) * (2 * WID)
                    pair = abuf[j, :, pl.ds(pl.multiple_of(first, HEAD_DIM), 2 * WID)]
                    part = pair[:, (q % 2) * WID : (q % 2 + 1) * WID]
                    total = total + lax.dot_general(
                        nbuf[q, xx], part, (((1,), (1,)), ((), ())), preferred_element_type=jnp.float32
                    )
            mine = tslot_ref[...] == xz * 4 + 2 * p + j
            term = jnp.where(mine, total, 0.0).astype(jnp.bfloat16)
            dpart[0] = term if j == 0 else dpart[0] + term
        z1 = z + 1 - 2 * (z % 2)
        for s, to in enumerate((d_cross, dev(x, y, z1, k), dev(x, y, 3 - z, k))):
            rc(dpart.at[s], drecv.at[s], dss.at[s], ds_.at[s], to).start()
            got(drecv.at[s], ds_.at[s])
            dpart[s + 1] = dpart[s] + drecv[s]
        rows = lax.broadcasted_iota(jnp.int32, (2 * RANK, 2 * SLOTS * RANK), 0)
        cols = lax.broadcasted_iota(jnp.int32, (2 * RANK, 2 * SLOTS * RANK), 1)
        place_of = (rows == cols % RANK + RANK * (cols // (SLOTS * RANK))).astype(jnp.bfloat16)
        wide = jnp.dot(dpart[3], place_of, preferred_element_type=jnp.float32)
        slot_of = (lax.broadcasted_iota(jnp.int32, (TOK, 2 * SLOTS * RANK), 1) // RANK) % SLOTS
        spread[...] = jnp.where(slot_of == tslot_ref[...], wide, 0.0).astype(jnp.bfloat16)
        got(ubuf, us)

    def qkv(h):
        def part(q, carry):
            s = jnp.dot(nbuf[q, 0], wbuf[h, q, 0], preferred_element_type=jnp.float32)
            for xx in range(1, 4):
                s = s + jnp.dot(nbuf[q, xx], wbuf[h, q, xx], preferred_element_type=jnp.float32)
            acc[...] += s
            return carry

        acc[...] = jnp.zeros_like(acc)
        lax.fori_loop(0, 4, part, 0)
        lanes = pl.ds(pl.multiple_of(h * HEAD_DIM, HEAD_DIM), HEAD_DIM)
        half = SLOTS * RANK
        up_q = ubuf[:, 0, :, lanes].reshape(half, HEAD_DIM)
        up_v = ubuf[:, 1, :, lanes].reshape(half, HEAD_DIM)
        dq = jnp.dot(spread[:, :half], up_q, preferred_element_type=jnp.float32)
        dv = jnp.dot(spread[:, half:], up_v, preferred_element_type=jnp.float32)
        qbuf[h] = (acc[:, :HEAD_DIM] + adapter_scale * dq).astype(jnp.bfloat16)
        kvwin[h, TOK:, :HEAD_DIM] = acc[:, HEAD_DIM : 2 * HEAD_DIM].astype(jnp.bfloat16)
        kvwin[h, TOK:, HEAD_DIM:] = (acc[:, 2 * HEAD_DIM :] + adapter_scale * dv).astype(jnp.bfloat16)

        @pl.when(tok < 15)
        def _():
            yn, xn = (tok + 1) % 4, (tok + 1) // 4
            e = (yn // 2 + p) % 2
            rc(
                kvwin.at[h, TOK:],
                kvwin.at[h, 0:TOK],
                ss.at[11],
                rs.at[11, h],
                dev(xn, yn + e * (3 - 2 * yn), z, (p + e) % 2),
            ).start()

    def attend(h):
        @pl.when(tok > 0)
        def _():
            got(kvwin.at[h, 0:TOK], rs.at[11, h])

        def block(i, carry):
            r0 = pl.multiple_of(i * 128, 128)
            qi = qbuf[h, pl.ds(r0, 128), :]
            ki = kvwin[h, pl.ds(r0, BAND), :HEAD_DIM]
            vi = kvwin[h, pl.ds(r0, BAND), HEAD_DIM:]
            s = lax.dot_general(qi, ki, (((1,), (1,)), ((), ())), preferred_element_type=jnp.float32)
            s = s * (HEAD_DIM**-0.5)
            u = lax.broadcasted_iota(jnp.int32, (128, BAND), 1)
            r = lax.broadcasted_iota(jnp.int32, (128, BAND), 0)
            lo = lo_ref[pl.ds(r0, 128), :] - r0
            s = jnp.where((u >= lo) & (u <= r + TOK), s, masked_score)
            e = jnp.exp(s - jnp.max(s, axis=1, keepdims=True))
            total = jnp.sum(e, axis=1, keepdims=True)
            o = jnp.dot(e.astype(jnp.bfloat16), vi, preferred_element_type=jnp.float32)
            att[h, pl.ds(r0, 128), :] = (o / total).astype(jnp.bfloat16)
            return carry

        lax.fori_loop(0, 4, block, 0)
        lanes = pl.ds(pl.multiple_of(h * HEAD_DIM, HEAD_DIM), HEAD_DIM)
        moves = (
            (att.at[h], out_att.at[:, lanes]),
            (kvwin.at[h, 2 * TOK - KEEP :, 0:HEAD_DIM], out_k.at[:, lanes]),
            (kvwin.at[h, 2 * TOK - KEEP :, HEAD_DIM : 2 * HEAD_DIM], out_v.at[:, lanes]),
        )
        for n, (src, dst) in enumerate(moves):

            @pl.when(lane0)
            def _():
                pltpu.make_async_copy(src, dst, os_.at[n]).start()

            @pl.when(lane1)
            def _():
                rc(src, dst, oss.at[n], os_.at[n], d_swap).start()

    def round_(i, carry):
        @pl.when(i + 2 < HEADS_DEV)
        def _():
            w_own(i + 2)

        @pl.when(i < HEADS_DEV)
        def _():
            h = i
            own = wbuf.at[h, q_own, x]
            got(own, rs.at[10, h])
            rc(own, own, ss.at[0], rs.at[0, h], d_xp).start()
            rc(own, own, ss.at[1], rs.at[1, h], d_xm).start()
            rc(own, own, ss.at[2], rs.at[2, h], d_m).start()

        @pl.when((i >= 1) & (i < HEADS_DEV + 1))
        def _():
            h = i - 1
            got(wbuf.at[h, q_own, xm], rs.at[0, h])
            lower = wbuf.at[h, q_own, xm, 0 : WID // 2]
            rc(lower, lower, ss.at[3], rs.at[3, h], d_xp).start()
            got(wbuf.at[h, q_own, xp], rs.at[1, h])
            upper = wbuf.at[h, q_own, xp, WID // 2 : WID]
            rc(upper, upper, ss.at[4], rs.at[4, h], d_xm).start()
            other = wbuf.at[h, q_mate, x]
            got(other, rs.at[2, h])
            rc(other, other, ss.at[5], rs.at[5, h], d_xp).start()
            rc(other, other, ss.at[6], rs.at[6, h], d_xm).start()

        @pl.when((i >= 2) & (i < HEADS_DEV + 2))
        def _():
            h = i - 2
            got(wbuf.at[h, q_own, xf, 0 : WID // 2], rs.at[3, h])
            got(wbuf.at[h, q_own, xf, WID // 2 : WID], rs.at[4, h])
            far = wbuf.at[h, q_own, xf]
            rc(far, far, ss.at[7], rs.at[7, h], d_m).start()
            four = wbuf.at[h, q_own]
            rc(four, four, ss.at[8], rs.at[8, h], d_core).start()

        @pl.when((i >= 3) & (i < HEADS_DEV + 3))
        def _():
            h = i - 3
            got(wbuf.at[h, q_mate, xm], rs.at[5, h])
            got(wbuf.at[h, q_mate, xp], rs.at[6, h])
            got(wbuf.at[h, q_mate, xf], rs.at[7, h])
            four = wbuf.at[h, q_mate]
            rc(four, four, ss.at[9], rs.at[9, h], d_core).start()

        @pl.when(i == 0)
        def _():
            for b in range(2):
                got(nbuf.at[b, xz], ns.at[b])
            rc(nbuf.at[0:2, xz], nbuf.at[2:4, xz], nss.at[2], ns.at[2], d_cross).start()

        @pl.when(i == 1)
        def _():
            got(nbuf.at[2:4, xz], ns.at[2])
            rc(nbuf.at[:, xz], nbuf.at[:, xz], nss.at[3], ns.at[3], d_zp).start()
            rc(nbuf.at[:, xz], nbuf.at[:, xz], nss.at[4], ns.at[4], d_zm).start()

        @pl.when(i == 3)
        def _():
            below, above = (x + zm) % 4, (x + zp) % 4
            got(nbuf.at[:, below], ns.at[3])
            rc(nbuf.at[0:2, below], nbuf.at[0:2, below], nss.at[5], ns.at[5], d_zp).start()
            got(nbuf.at[:, above], ns.at[4])
            rc(nbuf.at[2:4, above], nbuf.at[2:4, above], nss.at[6], ns.at[6], d_zm).start()

        @pl.when(i == 5)
        def _():
            opposite = (x + zf) % 4
            got(nbuf.at[0:2, opposite], ns.at[5])
            got(nbuf.at[2:4, opposite], ns.at[6])
            for b in range(2):
                got(abuf.at[b], as_.at[b])
            down()

        @pl.when((i >= 6) & (i < HEADS_DEV + 5))
        def _():
            def one(h, c):
                attend(h)
                return c

            lax.fori_loop(i - 5 - 6 // i, i - 4, one, 0)

        @pl.when((i >= 5) & (i < HEADS_DEV + 4))
        def _():
            def one(h, c):
                got(wbuf.at[h, o_own], rs.at[8, h])
                got(wbuf.at[h, o_mate], rs.at[9, h])
                qkv(h)
                return c

            lax.fori_loop(i - 4 - 5 // i, i - 3, one, 0)

        return carry

    lax.fori_loop(0, HEADS_DEV + 5, round_, 0)

    for n in (0, 1, 2, 5, 6, 7):
        sent(wbuf.at[:, 0, 0], ss.at[n])
    for n in (3, 4):
        sent(wbuf.at[:, 0, 0, 0 : WID // 2], ss.at[n])
    for n in (8, 9):
        sent(wbuf.at[:, 0], ss.at[n])

    @pl.when(tok < 15)
    def _():
        sent(kvwin.at[:, 0:TOK], ss.at[11])

    @pl.when(z != 0)
    def _():
        sent(stage.at[0], nss.at[0])
        sent(abuf.at[0], ass.at[0])

    sent(stage.at[1], nss.at[1])
    sent(abuf.at[0], ass.at[1])
    sent(nbuf.at[0:2, 0], nss.at[2])
    sent(nbuf.at[:, 0], nss.at[3])
    sent(nbuf.at[:, 0], nss.at[4])
    sent(nbuf.at[0:2, 0], nss.at[5])
    sent(nbuf.at[0:2, 0], nss.at[6])
    for s in range(3):
        sent(dpart.at[s], dss.at[s])

    @pl.when(lane0)
    def _():
        sent(ubuf, uss)

    @pl.when(lane1)
    def _():
        sent(wbuf.at[:, 0, 0], ss.at[10])
        sent(out_att, oss.at[0])
        sent(out_k, oss.at[1])
        sent(out_v, oss.at[2])

    got(out_att, os_.at[0])
    got(out_k, os_.at[1])
    got(out_v, os_.at[2])


def run_fused(nt, w, at, up, tslot, lo):
    bf, f32 = jnp.bfloat16, jnp.float32
    dma = pltpu.SemaphoreType.DMA
    any_ = pl.BlockSpec(memory_space=pl.ANY)
    vmem = pl.BlockSpec(memory_space=pltpu.VMEM)
    wide = HEADS_DEV * HEAD_DIM
    return pl.pallas_call(
        fused,
        out_shape=(
            jax.ShapeDtypeStruct((TOK, wide), bf),
            jax.ShapeDtypeStruct((KEEP, wide), bf),
            jax.ShapeDtypeStruct((KEEP, wide), bf),
        ),
        in_specs=[any_, any_, any_, any_, vmem, vmem],
        out_specs=(any_, any_, any_),
        scratch_shapes=[
            pltpu.VMEM((HEADS_DEV, 4, 4, WID, 3 * HEAD_DIM), bf),
            pltpu.VMEM((4, 4, TOK, WID), bf),
            pltpu.VMEM((2, 2 * RANK, 16 * WID), bf),
            pltpu.VMEM((SLOTS, 2, RANK, wide), bf),
            pltpu.VMEM((2, WID, TOK), bf),
            pltpu.VMEM((2, TOK, WID), bf),
            pltpu.VMEM((HEADS_DEV, 2 * TOK, 2 * HEAD_DIM), bf),
            pltpu.VMEM((HEADS_DEV, TOK, HEAD_DIM), bf),
            pltpu.VMEM((HEADS_DEV, TOK, HEAD_DIM), bf),
            pltpu.VMEM((TOK, 3 * HEAD_DIM), f32),
            pltpu.VMEM((4, TOK, 2 * RANK), bf),
            pltpu.VMEM((3, TOK, 2 * RANK), bf),
            pltpu.VMEM((TOK, 2 * SLOTS * RANK), bf),
            dma((12, HEADS_DEV)),
            dma((12,)),
            dma((7,)),
            dma((7,)),
            dma((2,)),
            dma((2,)),
            dma((3,)),
            dma((3,)),
            dma,
            dma,
            dma((2,)),
            dma((3,)),
            dma((3,)),
        ],
        compiler_params=pltpu.CompilerParams(has_side_effects=True, vmem_limit_bytes=67_043_328),
    )(nt, w, at, up, tslot, lo)


def local(
    normed,
    projection_weight,
    adapter_down_weight,
    adapter_up_weight,
    packed_prompt_length,
    prompt_adapter_ids,
    slot_adapter_ids,
    prompt_page_slots,
):
    col = lax.axis_index("col")
    tok = place()[-1]
    ends = jnp.cumsum(packed_prompt_length)
    starts = ends - packed_prompt_length
    matched = slot_adapter_ids[None, :] == prompt_adapter_ids[:, None]
    slot_of = jnp.sum(jnp.where(matched, jnp.arange(SLOTS, dtype=jnp.int32)[None, :], 0), axis=1)
    positions = tok * TOK + jnp.arange(TOK, dtype=jnp.int32)
    inside = (positions[:, None] >= starts[None, :]) & (positions[:, None] < ends[None, :])
    tslot = jnp.sum(jnp.where(inside, slot_of[None, :], 0), axis=1, keepdims=True)
    first = jnp.sum(jnp.where(inside, starts[None, :], 0), axis=1, keepdims=True)
    lo = first - (tok * TOK - TOK)
    attended, keys, values = run_fused(
        normed.T,
        jnp.transpose(projection_weight, (1, 0, 2)),
        jnp.transpose(adapter_down_weight, (1, 2, 0))[0],
        adapter_up_weight,
        tslot,
        lo,
    )
    window = jnp.pad(jnp.stack([keys, values], axis=1), ((0, PAGE), (0, 0), (0, 0)))
    pages = prompt_page_slots.shape[1]
    page_index = jnp.arange(pages, dtype=jnp.int32)
    page_rows = jnp.clip(packed_prompt_length[:, None] - PAGE * page_index[None, :], 0, PAGE)
    page_first = starts[:, None] + PAGE * page_index[None, :]
    my_slots = col * SLOTS_DEV + jnp.arange(SLOTS_DEV, dtype=jnp.int32)
    hit = prompt_page_slots.reshape(-1)[None, :] == my_slots[:, None]
    used = jnp.sum(jnp.where(hit, page_rows.reshape(-1)[None, :], 0), axis=1)
    first_used = jnp.sum(jnp.where(hit, page_first.reshape(-1)[None, :], 0), axis=1)
    offset = jnp.clip(first_used - (col * TOK + TOK - KEEP), 0, KEEP)
    lines = jnp.arange(PAGE, dtype=jnp.int32)
    out = []
    for i in range(SLOTS_DEV):
        rows = lax.dynamic_slice_in_dim(window, offset[i], PAGE, 0)
        out.append(jnp.where((lines < used[i])[:, None, None], rows, jnp.zeros_like(rows)))
    return attended, jnp.stack(out)


def solution(mesh):
    placed = (
        P(None, "col"),
        P("col", None, "row"),
        P(None, "col", None),
        P(None, None, None, "row"),
        P(),
        P(),
        P(),
        P(),
    )
    return jax.shard_map(
        local,
        mesh=mesh,
        in_specs=placed,
        out_specs=(P("col", "row"), P("col", None, None, "row")),
        check_vma=False,
    )
```

```python
import jax
import jax.numpy as jnp
from jax import lax
from jax.experimental import pallas as pl
from jax.experimental.pallas import tpu as pltpu
from jax.sharding import PartitionSpec as P

HEAD_DIM = 128
PAGE = 128
SLOTS_DEV = 10
HEADS_DEV = 7
SLOTS = 16
RANK = 16
TOK = 512
WID = 448
KEEP = 640
BAND = 640
PROMPTS = 64
QUARTER = 128
FAR = 128
VIA = 400

adapter_scale = 2.0
masked_score = -1e30
MESH = pl.DeviceIdType.MESH


def place():
    col = lax.axis_index("col")
    row = lax.axis_index("row")
    x, y = col // 4, col % 4
    z, k = row // 2, row % 2
    p = y // 2
    d = (k + p) % 2
    tok = x * 4 + y + d * (3 - 2 * y)
    return x, y, z, k, p, d, tok


def dev(x, y, z, k):
    return (z * 2 + k, x * 4 + y)


def holder(t, z, p):
    x, y = t // 4, t % 4
    e = (y // 2 + p) % 2
    return dev(x, y + e * (3 - 2 * y), z, (p + e) % 2)


def to_column(line, n):
    r = lax.broadcasted_iota(jnp.int32, (n, n), 0)
    c = lax.broadcasted_iota(jnp.int32, (n, n), 1)
    return jnp.sum(jnp.where(r == c, line, 0.0), axis=1, keepdims=True)


def fused(
    nt_ref,
    w_ref,
    at_ref,
    up_ref,
    len_ref,
    ask_ref,
    slot_ref,
    page_ref,
    out_att,
    out_k,
    out_v,
    out_page,
    wbuf,
    nbuf,
    abuf,
    ubuf,
    raw,
    stage,
    kvwin,
    qbuf,
    att,
    acc,
    dpart,
    drecv,
    spread,
    tslot,
    low,
    rs,
    ss,
    ns,
    nss,
    as_,
    ass,
    ds_,
    dss,
    us,
    uss,
    raws,
    os_,
    oss,
):
    x, y, z, k, p, d, tok = place()
    xp, xm, xf = (x + 1) % 4, (x + 3) % 4, (x + 2) % 4
    zp, zm, zf = (z + 1) % 4, (z + 3) % 4, (z + 2) % 4
    mate = y + 1 - 2 * (y % 2)
    d_xp = dev(xp, y, z, k)
    d_xm = dev(xm, y, z, k)
    d_m = dev(x, mate, z, k)
    d_core = dev(x, y, z, 1 - k)
    d_swap = dev(x, 3 - y, z, 1 - k)
    d_cross = dev(x, 3 - y, z, k)
    d_zp = dev(x, y, zp, k)
    d_zm = dev(x, y, zm, k)
    b_own = (y + d) % 2
    q_own = 2 * d + b_own
    q_mate = 2 * d + 1 - b_own
    o_own = 2 * (1 - d) + (y + 1 - d) % 2
    o_mate = 2 * (1 - d) + 1 - (y + 1 - d) % 2
    lane0 = d == 0
    lane1 = d == 1
    b_src = y % 2

    def rc(src, dst, send, recv, to):
        return pltpu.make_async_remote_copy(
            src_ref=src, dst_ref=dst, send_sem=send, recv_sem=recv, device_id=to, device_id_type=MESH
        )

    def got(ref, sem):
        rc(ref, ref, ss.at[0], sem, d_core).wait_recv()

    def sent(ref, sem):
        rc(ref, ref, sem, rs.at[0, 0], d_core).wait_send()

    barrier = pltpu.get_barrier_semaphore()

    def greet(to):
        pl.semaphore_signal(barrier, inc=1, device_id=to, device_id_type=MESH)

    near = [d_core, d_swap, d_cross, d_zp, d_zm, d_m]
    for xt in (xp, xm, xf):
        near += [dev(xt, y, z, k), dev(xt, mate, z, k)]
    for to in near:
        greet(to)

    greet(holder((tok + 1) % 16, z, p))
    greet(holder((tok + 15) % 16, z, p))
    pl.semaphore_wait(barrier, len(near) + 2)

    def w_own(h):
        for j in range(3):
            src = w_ref.at[j, :, pl.ds(pl.multiple_of(h * HEAD_DIM, HEAD_DIM), HEAD_DIM)]
            lanes = pl.ds(j * HEAD_DIM, HEAD_DIM)

            @pl.when(lane0)
            def _():
                pltpu.make_async_copy(src, wbuf.at[h, q_own, x, :, lanes], rs.at[10, h]).start()

            @pl.when(lane1)
            def _():
                rc(src, wbuf.at[h, 2 + b_src, x, :, lanes], ss.at[10], rs.at[10, h], d_swap).start()

    def w_first(h):
        own = wbuf.at[h, q_own, x]
        got(own, rs.at[10, h])
        rc(own, own, ss.at[0], rs.at[0, h], d_xp).start()
        rc(own, own, ss.at[1], rs.at[1, h], d_xm).start()
        rc(own, own, ss.at[2], rs.at[2, h], d_m).start()

    def block_of(n):
        xt = n // 2
        yt = y + (n % 2) * (mate - y)
        tt = xt * 4 + yt + d * (3 - 2 * yt)
        first = pl.multiple_of(tt * TOK + z * QUARTER, QUARTER)
        return xt, yt, pltpu.make_async_copy(
            nt_ref.at[:, pl.ds(first, QUARTER)], raw.at[n], raws.at[n]
        )

    def load(n, c):
        block_of(n)[2].start()
        return c

    lax.fori_loop(0, 8, load, 0)
    w_own(0)
    w_own(1)
    w_own(2)
    mine = pl.ds(pl.multiple_of(z * QUARTER, QUARTER), QUARTER)
    ranks = pl.ds(pl.multiple_of(z * 8, 8), 8)

    def scatter(n, c):
        xt, yt, copy = block_of(n)
        copy.wait()
        stage[n] = raw[n].T
        itself = (xt == x) & (n % 2 == 0)

        @pl.when(itself)
        def _():
            pltpu.make_async_copy(stage.at[n], nbuf.at[b_src, x, mine], ns.at[0]).start()

        @pl.when(jnp.logical_not(itself))
        def _():
            rc(stage.at[n], nbuf.at[b_src, x, mine], nss.at[0], ns.at[0], dev(xt, yt, z, k)).start()

        @pl.when((b_src == k) & itself)
        def _():
            pltpu.make_async_copy(at_ref.at[ranks], abuf.at[b_src, x], as_.at[0]).start()

        @pl.when((b_src == k) & jnp.logical_not(itself))
        def _():
            rc(at_ref.at[ranks], abuf.at[b_src, x], ass.at[0], as_.at[0], dev(xt, yt, z, k)).start()

        return c

    @pl.when(lane0)
    def _():
        w_first(0)

    lax.fori_loop(0, 8, scatter, 0)

    @pl.when(lane1)
    def _():
        w_first(0)

    @pl.when(lane0)
    def _():
        pltpu.make_async_copy(up_ref, ubuf, us).start()
        rc(up_ref, ubuf, uss, us, d_core).start()

    @pl.when(tok == 0)
    def _():
        kvwin[:, 0:TOK, :] = jnp.zeros((HEADS_DEV, TOK, 2 * HEAD_DIM), jnp.bfloat16)

    f32 = jnp.float32
    lens = len_ref[...].astype(f32)
    r64 = lax.broadcasted_iota(jnp.int32, (PROMPTS, PROMPTS), 0)
    c64 = lax.broadcasted_iota(jnp.int32, (PROMPTS, PROMPTS), 1)
    starts = jnp.sum(jnp.where(r64 < c64, to_column(lens, PROMPTS), 0.0), axis=0, keepdims=True)
    slot_col = to_column(slot_ref[...].astype(f32), SLOTS)
    s_row = lax.broadcasted_iota(jnp.int32, (SLOTS, PROMPTS), 0)
    slot_of = jnp.sum(
        jnp.where(slot_col == ask_ref[...].astype(f32), s_row.astype(f32), 0.0), axis=0, keepdims=True
    )
    at = (lax.broadcasted_iota(jnp.int32, (TOK, PROMPTS), 0) + tok * TOK).astype(f32)
    inside = (at >= starts) & (at < starts + lens)
    tslot[...] = jnp.sum(jnp.where(inside, slot_of, 0.0), axis=1, keepdims=True).astype(jnp.int32)
    first = jnp.sum(jnp.where(inside, starts, 0.0), axis=1, keepdims=True).astype(jnp.int32)
    low[...] = first - (tok - 1) * TOK
    my_col = x * 4 + y
    where_ = s_row + my_col * SLOTS_DEV
    offset = jnp.zeros((SLOTS, 1), f32)
    used = jnp.zeros((SLOTS, 1), f32)
    for j in range(page_ref.shape[0]):
        hit = page_ref[j : j + 1, :] == where_
        offset += jnp.sum(jnp.where(hit, starts + float(PAGE * j), 0.0), axis=1, keepdims=True)
        used += jnp.sum(
            jnp.where(hit, jnp.clip(lens - float(PAGE * j), 0.0, float(PAGE)), 0.0), axis=1, keepdims=True
        )
    base = my_col * TOK + TOK - KEEP
    offset = jnp.clip(offset.astype(jnp.int32) - base, 0, KEEP - 1)
    lane = lax.broadcasted_iota(jnp.int32, (SLOTS, 128), 1)
    out_page[...] = jnp.where(lane == 0, offset, used.astype(jnp.int32))

    def down():
        total = jnp.zeros((TOK, 64), f32)
        for q in range(4):
            for xx in range(4):
                begin = (xx * 2 + (p + q // 2) % 2) * (2 * WID)
                pair = abuf[:, :, :, pl.ds(pl.multiple_of(begin, HEAD_DIM), 2 * WID)].reshape(64, 2 * WID)
                part = pair[:, (q % 2) * WID : (q % 2 + 1) * WID]
                total = total + lax.dot_general(
                    nbuf[q, xx], part, (((1,), (1,)), ((), ())), preferred_element_type=f32
                )
        n = lax.broadcasted_iota(jnp.int32, (TOK, 64), 1)
        slot = ((n // 8) % 4) * 4 + 2 * p + n // 32
        term = jnp.where(slot == tslot[...], total, 0.0).astype(jnp.bfloat16)
        rows = lax.broadcasted_iota(jnp.int32, (64, 2 * RANK), 0)
        cols = lax.broadcasted_iota(jnp.int32, (64, 2 * RANK), 1)
        fold = (cols == rows % 8 + 8 * z).astype(jnp.bfloat16)
        dpart[0] = jnp.dot(term, fold, preferred_element_type=f32).astype(jnp.bfloat16)
        z1 = z + 1 - 2 * (z % 2)
        for s, to in enumerate((d_cross, dev(x, y, z1, k), dev(x, y, 3 - z, k))):
            rc(dpart.at[s], drecv.at[s], dss.at[s], ds_.at[s], to).start()
            got(drecv.at[s], ds_.at[s])
            dpart[s + 1] = dpart[s] + drecv[s]
        rows = lax.broadcasted_iota(jnp.int32, (2 * RANK, 2 * SLOTS * RANK), 0)
        cols = lax.broadcasted_iota(jnp.int32, (2 * RANK, 2 * SLOTS * RANK), 1)
        place_of = (rows == cols % RANK + RANK * (cols // (SLOTS * RANK))).astype(jnp.bfloat16)
        wide = jnp.dot(dpart[3], place_of, preferred_element_type=f32)
        slot_at = (lax.broadcasted_iota(jnp.int32, (TOK, 2 * SLOTS * RANK), 1) // RANK) % SLOTS
        spread[...] = jnp.where(slot_at == tslot[...], wide, 0.0).astype(jnp.bfloat16)
        got(ubuf, us)

    def head_lanes(h):
        return pl.ds(pl.multiple_of(h * HEAD_DIM, HEAD_DIM), HEAD_DIM)

    def deliver(moves):
        for src, dst, n in moves:

            @pl.when(lane0)
            def _():
                pltpu.make_async_copy(src, dst, os_.at[n]).start()

            @pl.when(lane1)
            def _():
                rc(src, dst, oss.at[n], os_.at[n], d_swap).start()

    def qkv(h, n):
        def part(q):
            s = jnp.dot(nbuf[q, 0], wbuf[h, q, 0], preferred_element_type=f32)
            for xx in range(1, 4):
                s = s + jnp.dot(nbuf[q, xx], wbuf[h, q, xx], preferred_element_type=f32)
            acc[...] += s

        def theirs(own):
            return own * o_own + (1 - own) * o_mate

        @pl.when(n == 0)
        def _():
            acc[...] = jnp.zeros_like(acc)

        part((1 - n) * q_own + n * q_mate)
        got(wbuf.at[h, theirs(1 - n)], rs.at[8 + n, h])
        part(theirs(1 - n))

        @pl.when(n == 1)
        def _():
            finish(h)

    def finish(h):
        lanes = pl.ds(pl.multiple_of(h * HEAD_DIM, HEAD_DIM), HEAD_DIM)
        half = SLOTS * RANK
        up_q = ubuf[:, 0, :, lanes].reshape(half, HEAD_DIM)
        up_v = ubuf[:, 1, :, lanes].reshape(half, HEAD_DIM)
        dq = jnp.dot(spread[:, :half], up_q, preferred_element_type=f32)
        dv = jnp.dot(spread[:, half:], up_v, preferred_element_type=f32)
        qbuf[h] = (acc[:, :HEAD_DIM] + adapter_scale * dq).astype(jnp.bfloat16)
        kvwin[h, TOK:, :HEAD_DIM] = acc[:, HEAD_DIM : 2 * HEAD_DIM].astype(jnp.bfloat16)
        kvwin[h, TOK:, HEAD_DIM:] = (acc[:, 2 * HEAD_DIM :] + adapter_scale * dv).astype(jnp.bfloat16)

        @pl.when(tok < 15)
        def _():
            rc(
                kvwin.at[h, TOK:], kvwin.at[h, 0:TOK], ss.at[11], rs.at[11, h], holder(tok + 1, z, p)
            ).start()

        deliver(
            (
                (kvwin.at[h, TOK:, 0:HEAD_DIM], out_k.at[KEEP - TOK :, head_lanes(h)], 1),
                (kvwin.at[h, TOK:, HEAD_DIM:], out_v.at[KEEP - TOK :, head_lanes(h)], 2),
            )
        )

    def attend(h):
        @pl.when(tok > 0)
        def _():
            got(kvwin.at[h, 0:TOK], rs.at[11, h])

        def block(i, carry):
            r0 = pl.multiple_of(i * 128, 128)
            qi = qbuf[h, pl.ds(r0, 128), :]
            ki = kvwin[h, pl.ds(r0, BAND), :HEAD_DIM]
            vi = kvwin[h, pl.ds(r0, BAND), HEAD_DIM:]
            s = lax.dot_general(qi, ki, (((1,), (1,)), ((), ())), preferred_element_type=f32)
            s = s * (HEAD_DIM**-0.5)
            u = lax.broadcasted_iota(jnp.int32, (128, BAND), 1)
            r = lax.broadcasted_iota(jnp.int32, (128, BAND), 0)
            lo = low[pl.ds(r0, 128), :] - r0
            s = jnp.where((u >= lo) & (u <= r + TOK), s, masked_score)
            e = jnp.exp(s - jnp.max(s, axis=1, keepdims=True))
            total = jnp.sum(e, axis=1, keepdims=True)
            o = jnp.dot(e.astype(jnp.bfloat16), vi, preferred_element_type=f32)
            att[h, pl.ds(r0, 128), :] = (o / total).astype(jnp.bfloat16)
            return carry

        early = pl.ds(2 * TOK - KEEP, KEEP - TOK)
        deliver(
            (
                (kvwin.at[h, early, 0:HEAD_DIM], out_k.at[0 : KEEP - TOK, head_lanes(h)], 1),
                (kvwin.at[h, early, HEAD_DIM:], out_v.at[0 : KEEP - TOK, head_lanes(h)], 2),
            )
        )
        lax.fori_loop(0, 4, block, 0)
        deliver(((att.at[h], out_att.at[:, head_lanes(h)], 0),))

    def tokens_of(zz):
        return pl.ds(pl.multiple_of(zz * QUARTER, QUARTER), QUARTER)

    def round_(i, carry):
        @pl.when(i + 3 < HEADS_DEV)
        def _():
            w_own(i + 3)

        @pl.when(i + 1 < HEADS_DEV)
        def _():
            w_first(i + 1)

        @pl.when(i < HEADS_DEV)
        def _():
            h = i
            got(wbuf.at[h, q_own, xm], rs.at[0, h])
            lower = wbuf.at[h, q_own, xm, 0:FAR]
            rc(lower, lower, ss.at[3], rs.at[3, h], d_xp).start()
            rest = wbuf.at[h, q_own, xm, VIA:WID]
            rc(rest, rest, ss.at[12], rs.at[12, h], d_m).start()
            got(wbuf.at[h, q_own, xp], rs.at[1, h])
            upper = wbuf.at[h, q_own, xp, FAR:WID]
            rc(upper, upper, ss.at[4], rs.at[4, h], d_xm).start()
            rest = wbuf.at[h, q_own, xp, VIA:WID]
            rc(rest, rest, ss.at[13], rs.at[13, h], d_m).start()
            got(wbuf.at[h, q_mate, x], rs.at[2, h])
            other = wbuf.at[h, q_mate, x, 0:VIA]
            rc(other, other, ss.at[5], rs.at[5, h], d_xp).start()
            rc(other, other, ss.at[6], rs.at[6, h], d_xm).start()

        @pl.when((i >= 1) & (i < HEADS_DEV + 1))
        def _():
            h = i - 1
            got(wbuf.at[h, q_own, xf, 0:FAR], rs.at[3, h])
            got(wbuf.at[h, q_own, xf, FAR:WID], rs.at[4, h])
            far = wbuf.at[h, q_own, xf]
            rc(far, far, ss.at[7], rs.at[7, h], d_m).start()
            four = wbuf.at[h, q_own]
            rc(four, four, ss.at[8], rs.at[8, h], d_core).start()

        @pl.when(i == 0)
        def _():
            got(nbuf.at[0:2, :, mine], ns.at[0])
            u = nbuf.at[0:2, :, mine]
            rc(u, nbuf.at[2:4, :, mine], nss.at[1], ns.at[1], d_cross).start()
            rc(u, u, nss.at[2], ns.at[2], d_zp).start()
            rc(u, u, nss.at[3], ns.at[3], d_zm).start()
            got(abuf.at[k], as_.at[0])
            rc(abuf.at[k], abuf.at[k], ass.at[1], as_.at[1], d_core).start()

        @pl.when(i == 2)
        def _():
            u = nbuf.at[2:4, :, mine]
            got(u, ns.at[1])
            rc(u, u, nss.at[4], ns.at[4], d_zp).start()
            rc(u, u, nss.at[5], ns.at[5], d_zm).start()
            got(nbuf.at[0:2, :, tokens_of(zm)], ns.at[2])
            u = nbuf.at[0, :, tokens_of(zm)]
            rc(u, u, nss.at[6], ns.at[6], d_zp).start()
            got(nbuf.at[0:2, :, tokens_of(zp)], ns.at[3])
            u = nbuf.at[1, :, tokens_of(zp)]
            rc(u, u, nss.at[7], ns.at[7], d_zm).start()

        @pl.when(i == 3)
        def _():
            got(nbuf.at[2:4, :, tokens_of(zm)], ns.at[4])
            u = nbuf.at[2, :, tokens_of(zm)]
            rc(u, u, nss.at[8], ns.at[8], d_zp).start()
            got(nbuf.at[2:4, :, tokens_of(zp)], ns.at[5])
            u = nbuf.at[3, :, tokens_of(zp)]
            rc(u, u, nss.at[9], ns.at[9], d_zm).start()

        @pl.when(i == 4)
        def _():
            for q in range(4):
                got(nbuf.at[q, :, tokens_of(zf)], ns.at[6 + q])
            got(abuf.at[1 - k], as_.at[1])
            down()

        @pl.when(i >= 5)
        def _():
            def one(h, c):
                attend(h)
                return c

            lax.fori_loop(i - 4 - 6 // i, i - 3 - 6 // (i + 1), one, 0)

        def first_step(i):
            return 2 * i - 5 - 6 // i - 2 * (5 // i)

        @pl.when((i >= 4) & (i < HEADS_DEV + 3))
        def _():
            def one(step, c):
                @pl.when(step < 2 * HEADS_DEV)
                def _():
                    qkv(step // 2, step % 2)

                return c

            lax.fori_loop(first_step(i), first_step(i + 1), one, 0)

        @pl.when((i >= 2) & (i < HEADS_DEV + 2))
        def _():
            h = i - 2
            got(wbuf.at[h, q_mate, xm, 0:VIA], rs.at[5, h])
            got(wbuf.at[h, q_mate, xp, 0:VIA], rs.at[6, h])
            got(wbuf.at[h, q_mate, xm, VIA:WID], rs.at[12, h])
            got(wbuf.at[h, q_mate, xp, VIA:WID], rs.at[13, h])
            got(wbuf.at[h, q_mate, xf], rs.at[7, h])
            four = wbuf.at[h, q_mate]
            rc(four, four, ss.at[9], rs.at[9, h], d_core).start()

        return carry

    lax.fori_loop(0, HEADS_DEV + 4, round_, 0)

    for n in (0, 1, 2, 7):
        sent(wbuf.at[:, 0, 0], ss.at[n])
    sent(wbuf.at[:, 0, 0, 0:FAR], ss.at[3])
    sent(wbuf.at[:, 0, 0, FAR:WID], ss.at[4])
    for n in (5, 6):
        sent(wbuf.at[:, 0, 0, 0:VIA], ss.at[n])
    for n in (12, 13):
        sent(wbuf.at[:, 0, 0, VIA:WID], ss.at[n])
    for n in (8, 9):
        sent(wbuf.at[:, 0], ss.at[n])

    @pl.when(tok < 15)
    def _():
        sent(kvwin.at[:, 0:TOK], ss.at[11])

    sent(stage.at[0:7], nss.at[0])
    for n in range(1, 6):
        sent(nbuf.at[0:2, :, mine], nss.at[n])
    for n in range(6, 10):
        sent(nbuf.at[0, :, mine], nss.at[n])

    @pl.when(b_src == k)
    def _():
        sent(w_ref.at[0], ass.at[0])

    sent(abuf.at[0], ass.at[1])
    for s in range(3):
        sent(dpart.at[s], dss.at[s])

    @pl.when(lane0)
    def _():
        sent(ubuf, uss)

    @pl.when(lane1)
    def _():
        sent(wbuf.at[:, 0, 0], ss.at[10])
        sent(out_att, oss.at[0])
        sent(out_k, oss.at[1])
        sent(out_v, oss.at[2])

    got(out_att, os_.at[0])
    got(out_k, os_.at[1])
    got(out_v, os_.at[2])


def run_fused(*operands):
    bf, f32, i32 = jnp.bfloat16, jnp.float32, jnp.int32
    dma = pltpu.SemaphoreType.DMA
    any_ = pl.BlockSpec(memory_space=pl.ANY)
    vmem = pl.BlockSpec(memory_space=pltpu.VMEM)
    wide = HEADS_DEV * HEAD_DIM
    return pl.pallas_call(
        fused,
        out_shape=(
            jax.ShapeDtypeStruct((TOK, wide), bf),
            jax.ShapeDtypeStruct((KEEP, wide), bf),
            jax.ShapeDtypeStruct((KEEP, wide), bf),
            jax.ShapeDtypeStruct((SLOTS, 128), i32),
        ),
        in_specs=[any_] * 4 + [vmem] * 4,
        out_specs=(any_, any_, any_, vmem),
        scratch_shapes=[
            pltpu.VMEM((HEADS_DEV, 4, 4, WID, 3 * HEAD_DIM), bf),
            pltpu.VMEM((4, 4, TOK, WID), bf),
            pltpu.VMEM((2, 4, 8, 16 * WID), bf),
            pltpu.VMEM((SLOTS, 2, RANK, wide), bf),
            pltpu.VMEM((8, WID, QUARTER), bf),
            pltpu.VMEM((8, QUARTER, WID), bf),
            pltpu.VMEM((HEADS_DEV, 2 * TOK, 2 * HEAD_DIM), bf),
            pltpu.VMEM((HEADS_DEV, TOK, HEAD_DIM), bf),
            pltpu.VMEM((HEADS_DEV, TOK, HEAD_DIM), bf),
            pltpu.VMEM((TOK, 3 * HEAD_DIM), f32),
            pltpu.VMEM((4, TOK, 2 * RANK), bf),
            pltpu.VMEM((3, TOK, 2 * RANK), bf),
            pltpu.VMEM((TOK, 2 * SLOTS * RANK), bf),
            pltpu.VMEM((TOK, 1), i32),
            pltpu.VMEM((TOK, 1), i32),
            dma((14, HEADS_DEV)),
            dma((14,)),
            dma((10,)),
            dma((10,)),
            dma((2,)),
            dma((2,)),
            dma((3,)),
            dma((3,)),
            dma,
            dma,
            dma((8,)),
            dma((3,)),
            dma((3,)),
        ],
        compiler_params=pltpu.CompilerParams(
            collective_id=0, has_side_effects=True, vmem_limit_bytes=67_043_328
        ),
    )(*operands)


def assemble(page_ref, k_ref, v_ref, out_ref):
    s = pl.program_id(0)
    offset, used = page_ref[s, 0], page_ref[s, 1]
    span = PAGE + 16
    first = jnp.minimum(offset // 16 * 16, KEEP - span)
    first = pl.multiple_of(first, 16)
    lines = jnp.concatenate([k_ref[pl.ds(first, span), :], v_ref[pl.ds(first, span), :]], axis=0)
    n = lax.broadcasted_iota(jnp.int32, (2 * PAGE, 2 * span), 0)
    m = lax.broadcasted_iota(jnp.int32, (2 * PAGE, 2 * span), 1)
    pick = (m == (n % 2) * span + n // 2 + (offset - first)) & (n // 2 < used)
    rows = jnp.dot(pick.astype(jnp.bfloat16), lines, preferred_element_type=jnp.float32)
    out_ref[0] = rows.astype(jnp.bfloat16).reshape(PAGE, 2, lines.shape[1])


def run_assemble(page, keys, values):
    wide = keys.shape[1]
    vmem = pl.BlockSpec(memory_space=pltpu.VMEM)
    return pl.pallas_call(
        assemble,
        grid=(SLOTS_DEV,),
        out_shape=jax.ShapeDtypeStruct((SLOTS_DEV, PAGE, 2, wide), keys.dtype),
        in_specs=[pl.BlockSpec(memory_space=pltpu.SMEM), vmem, vmem],
        out_specs=pl.BlockSpec((1, PAGE, 2, wide), lambda s: (s, 0, 0, 0)),
    )(page, keys, values)


def local(
    normed,
    projection_weight,
    adapter_down_weight,
    adapter_up_weight,
    packed_prompt_length,
    prompt_adapter_ids,
    slot_adapter_ids,
    prompt_page_slots,
):
    attended, keys, values, page = run_fused(
        normed.T,
        jnp.transpose(projection_weight, (1, 0, 2)),
        jnp.transpose(adapter_down_weight, (1, 2, 0))[0],
        adapter_up_weight,
        packed_prompt_length[None, :],
        prompt_adapter_ids[None, :],
        slot_adapter_ids[None, :],
        prompt_page_slots.T,
    )
    return attended, run_assemble(page, keys, values)


def solution(mesh):
    placed = (
        P(None, "col"),
        P("col", None, "row"),
        P(None, "col", None),
        P(None, None, None, "row"),
        P(),
        P(),
        P(),
        P(),
    )
    return jax.shard_map(
        local,
        mesh=mesh,
        in_specs=placed,
        out_specs=(P("col", "row"), P("col", None, None, "row")),
        check_vma=False,
    )
```

```python
import jax
import jax.numpy as jnp
from jax import lax
from jax.experimental import pallas as pl
from jax.experimental.pallas import tpu as pltpu
from jax.sharding import PartitionSpec as P

HEAD_DIM = 128
PAGE = 128
SLOTS_DEV = 10
PER_STEP = 2
HEADS_DEV = 7
KV_BLOCKS = 14
SLOTS = 16
RANK = 16
TOK = 512
WID = 448
KEEP = 640
BAND = 640
PROMPTS = 64
QUARTER = 128
FAR = 224
VIA = 432

adapter_scale = 2.0
masked_score = -1e30
MESH = pl.DeviceIdType.MESH


def place():
    col = lax.axis_index("col")
    row = lax.axis_index("row")
    x, y = col // 4, col % 4
    z, k = row // 2, row % 2
    p = y // 2
    d = (k + p) % 2
    tok = x * 4 + y + d * (3 - 2 * y)
    return x, y, z, k, p, d, tok


def dev(x, y, z, k):
    return (z * 2 + k, x * 4 + y)


def holder(t, z, p):
    x, y = t // 4, t % 4
    e = (y // 2 + p) % 2
    return dev(x, y + e * (3 - 2 * y), z, (p + e) % 2)


def to_column(line, n):
    r = lax.broadcasted_iota(jnp.int32, (n, n), 0)
    c = lax.broadcasted_iota(jnp.int32, (n, n), 1)
    return jnp.sum(jnp.where(r == c, line, 0.0), axis=1, keepdims=True)


def fused(
    nt_ref,
    w_ref,
    at_ref,
    up_ref,
    len_ref,
    ask_ref,
    slot_ref,
    page_ref,
    out_att,
    out_k,
    out_v,
    out_page,
    wbuf,
    nbuf,
    abuf,
    ubuf,
    raw,
    stage,
    kvwin,
    qbuf,
    att,
    acc,
    dpart,
    drecv,
    spread,
    tslot,
    low,
    rs,
    ss,
    ns,
    nss,
    as_,
    ass,
    ds_,
    dss,
    us,
    uss,
    raws,
    os_,
    oss,
):
    x, y, z, k, p, d, tok = place()
    xp, xm, xf = (x + 1) % 4, (x + 3) % 4, (x + 2) % 4
    zp, zm, zf = (z + 1) % 4, (z + 3) % 4, (z + 2) % 4
    mate = y + 1 - 2 * (y % 2)
    d_xp = dev(xp, y, z, k)
    d_xm = dev(xm, y, z, k)
    d_m = dev(x, mate, z, k)
    d_core = dev(x, y, z, 1 - k)
    d_swap = dev(x, 3 - y, z, 1 - k)
    d_cross = dev(x, 3 - y, z, k)
    d_zp = dev(x, y, zp, k)
    d_zm = dev(x, y, zm, k)
    b_own = (y + d) % 2
    q_own = 2 * d + b_own
    q_mate = 2 * d + 1 - b_own
    o_own = 2 * (1 - d) + (y + 1 - d) % 2
    o_mate = 2 * (1 - d) + 1 - (y + 1 - d) % 2
    lane0 = d == 0
    lane1 = d == 1
    b_src = y % 2

    def rc(src, dst, send, recv, to):
        return pltpu.make_async_remote_copy(
            src_ref=src, dst_ref=dst, send_sem=send, recv_sem=recv, device_id=to, device_id_type=MESH
        )

    def got(ref, sem):
        rc(ref, ref, ss.at[0], sem, d_core).wait_recv()

    def sent(ref, sem):
        rc(ref, ref, sem, rs.at[0, 0], d_core).wait_send()

    barrier = pltpu.get_barrier_semaphore()

    def greet(to):
        pl.semaphore_signal(barrier, inc=1, device_id=to, device_id_type=MESH)

    near = [d_core, d_swap, d_cross, d_zp, d_zm, d_m]
    for xt in (xp, xm, xf):
        near += [dev(xt, y, z, k), dev(xt, mate, z, k)]
    for to in near:
        greet(to)

    greet(holder((tok + 1) % 16, z, p))
    greet(holder((tok + 15) % 16, z, p))
    pl.semaphore_wait(barrier, len(near) + 2)

    def w_own(h):
        for j in range(3):
            g = 3 * h + j
            late = g // KV_BLOCKS
            kind = (1 + g % 2) * (1 - late)
            head = late * (g - KV_BLOCKS) + (1 - late) * (g // 2)
            src = w_ref.at[kind, :, pl.ds(pl.multiple_of(head * HEAD_DIM, HEAD_DIM), HEAD_DIM)]
            lanes = pl.ds(j * HEAD_DIM, HEAD_DIM)

            @pl.when(lane0)
            def _():
                pltpu.make_async_copy(src, wbuf.at[h, q_own, x, :, lanes], rs.at[10, h]).start()

            @pl.when(lane1)
            def _():
                rc(src, wbuf.at[h, 2 + b_src, x, :, lanes], ss.at[10], rs.at[10, h], d_swap).start()

    def w_first(h):
        own = wbuf.at[h, q_own, x]
        got(own, rs.at[10, h])
        rc(own, own, ss.at[0], rs.at[0, h], d_xp).start()
        rc(own, own, ss.at[1], rs.at[1, h], d_xm).start()
        rc(own, own, ss.at[2], rs.at[2, h], d_m).start()

    def block_of(n):
        xt = n // 2
        yt = y + (n % 2) * (mate - y)
        tt = xt * 4 + yt + d * (3 - 2 * yt)
        first = pl.multiple_of(tt * TOK + z * QUARTER, QUARTER)
        return xt, yt, first

    def loading(n):
        columns = pl.ds(block_of(n)[2], QUARTER)
        return pltpu.make_async_copy(nt_ref.at[:, columns], raw.at[n], raws.at[n])

    def load(n, c):
        loading(n).start()
        return c

    lax.fori_loop(0, 8, load, 0)
    w_own(0)
    w_own(1)
    w_own(2)
    mine = pl.ds(pl.multiple_of(z * QUARTER, QUARTER), QUARTER)
    ranks = pl.ds(pl.multiple_of(z * 8, 8), 8)

    def scatter(n, c):
        xt, yt, _ = block_of(n)
        loading(n).wait()
        stage[n] = raw[n].T
        itself = (xt == x) & (n % 2 == 0)

        @pl.when(itself)
        def _():
            pltpu.make_async_copy(stage.at[n], nbuf.at[b_src, x, mine], ns.at[0]).start()

        @pl.when(jnp.logical_not(itself))
        def _():
            rc(stage.at[n], nbuf.at[b_src, x, mine], nss.at[0], ns.at[0], dev(xt, yt, z, k)).start()

        return c

    @pl.when(lane0)
    def _():
        w_first(0)

    lax.fori_loop(0, 8, scatter, 0)

    @pl.when(lane1)
    def _():
        w_first(0)

    def maps(n, c):
        xt, yt, _ = block_of(n)
        itself = (xt == x) & (n % 2 == 0)

        @pl.when((b_src == k) & itself)
        def _():
            pltpu.make_async_copy(at_ref.at[ranks], abuf.at[b_src, x], as_.at[0]).start()

        @pl.when((b_src == k) & jnp.logical_not(itself))
        def _():
            rc(at_ref.at[ranks], abuf.at[b_src, x], ass.at[0], as_.at[0], dev(xt, yt, z, k)).start()

        return c

    lax.fori_loop(0, 8, maps, 0)

    @pl.when(lane0)
    def _():
        pltpu.make_async_copy(up_ref, ubuf, us).start()
        rc(up_ref, ubuf, uss, us, d_core).start()

    @pl.when(tok == 0)
    def _():
        kvwin[:, 0:TOK, :] = jnp.zeros((HEADS_DEV, TOK, 2 * HEAD_DIM), jnp.bfloat16)

    f32 = jnp.float32
    lens = len_ref[...].astype(f32)
    r64 = lax.broadcasted_iota(jnp.int32, (PROMPTS, PROMPTS), 0)
    c64 = lax.broadcasted_iota(jnp.int32, (PROMPTS, PROMPTS), 1)
    starts = jnp.sum(jnp.where(r64 < c64, to_column(lens, PROMPTS), 0.0), axis=0, keepdims=True)
    slot_col = to_column(slot_ref[...].astype(f32), SLOTS)
    s_row = lax.broadcasted_iota(jnp.int32, (SLOTS, PROMPTS), 0)
    slot_of = jnp.sum(
        jnp.where(slot_col == ask_ref[...].astype(f32), s_row.astype(f32), 0.0), axis=0, keepdims=True
    )
    at = (lax.broadcasted_iota(jnp.int32, (TOK, PROMPTS), 0) + tok * TOK).astype(f32)
    inside = (at >= starts) & (at < starts + lens)
    tslot[...] = jnp.sum(jnp.where(inside, slot_of, 0.0), axis=1, keepdims=True).astype(jnp.int32)
    first = jnp.sum(jnp.where(inside, starts, 0.0), axis=1, keepdims=True).astype(jnp.int32)
    low[...] = first - (tok - 1) * TOK
    my_col = x * 4 + y
    where_ = s_row + my_col * SLOTS_DEV
    offset = jnp.zeros((SLOTS, 1), f32)
    used = jnp.zeros((SLOTS, 1), f32)
    for j in range(page_ref.shape[0]):
        hit = page_ref[j : j + 1, :] == where_
        offset += jnp.sum(jnp.where(hit, starts + float(PAGE * j), 0.0), axis=1, keepdims=True)
        used += jnp.sum(
            jnp.where(hit, jnp.clip(lens - float(PAGE * j), 0.0, float(PAGE)), 0.0), axis=1, keepdims=True
        )
    base = my_col * TOK + TOK - KEEP
    offset = jnp.clip(offset.astype(jnp.int32) - base, 0, KEEP - 1)
    lane = lax.broadcasted_iota(jnp.int32, (SLOTS, 128), 1)
    out_page[...] = jnp.where(lane == 0, offset, used.astype(jnp.int32))

    def down():
        total = jnp.zeros((TOK, 64), f32)
        for q in range(4):
            for xx in range(4):
                begin = (xx * 2 + (p + q // 2) % 2) * (2 * WID)
                pair = abuf[:, :, :, pl.ds(pl.multiple_of(begin, HEAD_DIM), 2 * WID)].reshape(64, 2 * WID)
                part = pair[:, (q % 2) * WID : (q % 2 + 1) * WID]
                total = total + lax.dot_general(
                    nbuf[q, xx], part, (((1,), (1,)), ((), ())), preferred_element_type=f32
                )
        n = lax.broadcasted_iota(jnp.int32, (TOK, 64), 1)
        slot = ((n // 8) % 4) * 4 + 2 * p + n // 32
        term = jnp.where(slot == tslot[...], total, 0.0).astype(jnp.bfloat16)
        rows = lax.broadcasted_iota(jnp.int32, (64, 2 * RANK), 0)
        cols = lax.broadcasted_iota(jnp.int32, (64, 2 * RANK), 1)
        fold = (cols == rows % 8 + 8 * z).astype(jnp.bfloat16)
        dpart[0] = jnp.dot(term, fold, preferred_element_type=f32).astype(jnp.bfloat16)
        z1 = z + 1 - 2 * (z % 2)
        for s, to in enumerate((d_cross, dev(x, y, z1, k), dev(x, y, 3 - z, k))):
            rc(dpart.at[s], drecv.at[s], dss.at[s], ds_.at[s], to).start()
            if s < 2:
                mm(0, s)
            got(drecv.at[s], ds_.at[s])
            dpart[s + 1] = dpart[s] + drecv[s]
        rows = lax.broadcasted_iota(jnp.int32, (2 * RANK, 2 * SLOTS * RANK), 0)
        cols = lax.broadcasted_iota(jnp.int32, (2 * RANK, 2 * SLOTS * RANK), 1)
        place_of = (rows == cols % RANK + RANK * (cols // (SLOTS * RANK))).astype(jnp.bfloat16)
        wide = jnp.dot(dpart[3], place_of, preferred_element_type=f32)
        slot_at = (lax.broadcasted_iota(jnp.int32, (TOK, 2 * SLOTS * RANK), 1) // RANK) % SLOTS
        spread[...] = jnp.where(slot_at == tslot[...], wide, 0.0).astype(jnp.bfloat16)
        got(ubuf, us)
        finish(0)

    def head_lanes(h):
        return pl.ds(pl.multiple_of(h * HEAD_DIM, HEAD_DIM), HEAD_DIM)

    def deliver(moves):
        for src, dst, n in moves:

            @pl.when(lane0)
            def _():
                pltpu.make_async_copy(src, dst, os_.at[n]).start()

            @pl.when(lane1)
            def _():
                rc(src, dst, oss.at[n], os_.at[n], d_swap).start()

    def mm(h, n):
        def part(q):
            s = jnp.dot(nbuf[q, 0], wbuf[h, q, 0], preferred_element_type=f32)
            for xx in range(1, 4):
                s = s + jnp.dot(nbuf[q, xx], wbuf[h, q, xx], preferred_element_type=f32)
            acc[...] += s

        def theirs(own):
            return own * o_own + (1 - own) * o_mate

        @pl.when(n == 0)
        def _():
            acc[...] = jnp.zeros_like(acc)

        part((1 - n) * q_own + n * q_mate)
        got(wbuf.at[h, theirs(1 - n)], rs.at[8 + n, h])
        part(theirs(1 - n))

    def qkv(h, n):
        mm(h, n)

        @pl.when(n == 1)
        def _():
            finish(h)

    def finish(r):
        half = SLOTS * RANK

        def one(j, carry):
            g = 3 * r + j
            block = acc.at[:, head_lanes(j)]

            @pl.when((g < KV_BLOCKS) & (g % 2 == 0))
            def _():
                kvwin[g // 2, TOK:, :HEAD_DIM] = block[...].astype(jnp.bfloat16)

            @pl.when((g < KV_BLOCKS) & (g % 2 == 1))
            def _():
                h = g // 2
                up_v = ubuf[:, 1, :, head_lanes(h)].reshape(half, HEAD_DIM)
                dv = jnp.dot(spread[:, half:], up_v, preferred_element_type=f32)
                kvwin[h, TOK:, HEAD_DIM:] = (block[...] + adapter_scale * dv).astype(jnp.bfloat16)

                @pl.when(tok < 15)
                def _():
                    mine_ = kvwin.at[h, TOK:]
                    theirs_ = kvwin.at[h, 0:TOK]
                    rc(mine_, theirs_, ss.at[11], rs.at[11, h], holder(tok + 1, z, p)).start()

                deliver(
                    (
                        (kvwin.at[h, TOK:, 0:HEAD_DIM], out_k.at[KEEP - TOK :, head_lanes(h)], 1),
                        (kvwin.at[h, TOK:, HEAD_DIM:], out_v.at[KEEP - TOK :, head_lanes(h)], 2),
                    )
                )

            @pl.when(g >= KV_BLOCKS)
            def _():
                h = g - KV_BLOCKS
                up_q = ubuf[:, 0, :, head_lanes(h)].reshape(half, HEAD_DIM)
                dq = jnp.dot(spread[:, :half], up_q, preferred_element_type=f32)
                qbuf[...] = (block[...] + adapter_scale * dq).astype(jnp.bfloat16)
                attend(h)

            return carry

        lax.fori_loop(0, 3, one, 0)

    def attend(h):
        @pl.when(tok > 0)
        def _():
            got(kvwin.at[h, 0:TOK], rs.at[11, h])

        early = pl.ds(2 * TOK - KEEP, KEEP - TOK)
        deliver(
            (
                (kvwin.at[h, early, 0:HEAD_DIM], out_k.at[0 : KEEP - TOK, head_lanes(h)], 1),
                (kvwin.at[h, early, HEAD_DIM:], out_v.at[0 : KEEP - TOK, head_lanes(h)], 2),
            )
        )
        for i in range(4):
            r0 = i * 128
            qi = qbuf[r0 : r0 + 128, :]
            ki = kvwin[h, r0 : r0 + BAND, :HEAD_DIM]
            vi = kvwin[h, r0 : r0 + BAND, HEAD_DIM:]
            s = lax.dot_general(qi, ki, (((1,), (1,)), ((), ())), preferred_element_type=f32)
            s = s * (HEAD_DIM**-0.5)
            u = lax.broadcasted_iota(jnp.int32, (128, BAND), 1)
            r = lax.broadcasted_iota(jnp.int32, (128, BAND), 0)
            lo = low[r0 : r0 + 128, :] - r0
            s = jnp.where((u >= lo) & (u <= r + TOK), s, masked_score)
            e = jnp.exp(s - jnp.max(s, axis=1, keepdims=True))
            total = jnp.sum(e, axis=1, keepdims=True)
            o = jnp.dot(e.astype(jnp.bfloat16), vi, preferred_element_type=f32)
            att[h, r0 : r0 + 128, :] = (o / total).astype(jnp.bfloat16)

        deliver(((att.at[h], out_att.at[:, head_lanes(h)], 0),))

    def tokens_of(zz):
        return pl.ds(pl.multiple_of(zz * QUARTER, QUARTER), QUARTER)

    def round_(i, carry):
        @pl.when(i + 3 < HEADS_DEV)
        def _():
            w_own(i + 3)

        @pl.when(i + 1 < HEADS_DEV)
        def _():
            w_first(i + 1)

        @pl.when(i < HEADS_DEV)
        def _():
            h = i
            got(wbuf.at[h, q_own, xm], rs.at[0, h])
            lower = wbuf.at[h, q_own, xm, 0:FAR]
            rc(lower, lower, ss.at[3], rs.at[3, h], d_xp).start()
            rest = wbuf.at[h, q_own, xm, VIA:WID]
            rc(rest, rest, ss.at[12], rs.at[12, h], d_m).start()
            got(wbuf.at[h, q_own, xp], rs.at[1, h])
            upper = wbuf.at[h, q_own, xp, FAR:WID]
            rc(upper, upper, ss.at[4], rs.at[4, h], d_xm).start()
            rest = wbuf.at[h, q_own, xp, VIA:WID]
            rc(rest, rest, ss.at[13], rs.at[13, h], d_m).start()
            got(wbuf.at[h, q_mate, x], rs.at[2, h])
            other = wbuf.at[h, q_mate, x, 0:VIA]
            rc(other, other, ss.at[5], rs.at[5, h], d_xp).start()
            rc(other, other, ss.at[6], rs.at[6, h], d_xm).start()

        @pl.when((i >= 1) & (i < HEADS_DEV + 1))
        def _():
            h = i - 1
            got(wbuf.at[h, q_own, xf, 0:FAR], rs.at[3, h])
            got(wbuf.at[h, q_own, xf, FAR:WID], rs.at[4, h])
            far = wbuf.at[h, q_own, xf]
            rc(far, far, ss.at[7], rs.at[7, h], d_m).start()
            four = wbuf.at[h, q_own]
            rc(four, four, ss.at[8], rs.at[8, h], d_core).start()

        @pl.when(i == 0)
        def _():
            got(nbuf.at[0:2, :, mine], ns.at[0])
            u = nbuf.at[0:2, :, mine]
            rc(u, nbuf.at[2:4, :, mine], nss.at[1], ns.at[1], d_cross).start()
            rc(u, u, nss.at[2], ns.at[2], d_zp).start()
            rc(u, u, nss.at[3], ns.at[3], d_zm).start()

        @pl.when(i == 2)
        def _():
            u = nbuf.at[2:4, :, mine]
            got(abuf.at[k], as_.at[0])
            rc(abuf.at[k], abuf.at[k], ass.at[1], as_.at[1], d_core).start()
            got(u, ns.at[1])
            rc(u, u, nss.at[4], ns.at[4], d_zp).start()
            rc(u, u, nss.at[5], ns.at[5], d_zm).start()
            got(nbuf.at[0:2, :, tokens_of(zm)], ns.at[2])
            u = nbuf.at[0, :, tokens_of(zm)]
            rc(u, u, nss.at[6], ns.at[6], d_zp).start()
            got(nbuf.at[0:2, :, tokens_of(zp)], ns.at[3])
            u = nbuf.at[1, :, tokens_of(zp)]
            rc(u, u, nss.at[7], ns.at[7], d_zm).start()

        @pl.when(i == 3)
        def _():
            got(nbuf.at[2:4, :, tokens_of(zm)], ns.at[4])
            u = nbuf.at[2, :, tokens_of(zm)]
            rc(u, u, nss.at[8], ns.at[8], d_zp).start()
            got(nbuf.at[2:4, :, tokens_of(zp)], ns.at[5])
            u = nbuf.at[3, :, tokens_of(zp)]
            rc(u, u, nss.at[9], ns.at[9], d_zm).start()

        @pl.when(i == 5)
        def _():
            for q in range(4):
                got(nbuf.at[q, :, tokens_of(zf)], ns.at[6 + q])
            got(abuf.at[1 - k], as_.at[1])
            down()

        def first_step(i):
            return 2 * i - 5 - 2 * (7 // i) - 2 * (6 // i) + (5 // i)

        @pl.when((i >= 5) & (i < HEADS_DEV + 3))
        def _():
            def one(step, c):
                @pl.when(step < 2 * HEADS_DEV)
                def _():
                    qkv(step // 2, step % 2)

                return c

            lax.fori_loop(first_step(i), first_step(i + 1), one, 0)

        @pl.when((i >= 2) & (i < HEADS_DEV + 2))
        def _():
            h = i - 2
            got(wbuf.at[h, q_mate, xm, 0:VIA], rs.at[5, h])
            got(wbuf.at[h, q_mate, xp, 0:VIA], rs.at[6, h])
            got(wbuf.at[h, q_mate, xm, VIA:WID], rs.at[12, h])
            got(wbuf.at[h, q_mate, xp, VIA:WID], rs.at[13, h])
            got(wbuf.at[h, q_mate, xf], rs.at[7, h])
            four = wbuf.at[h, q_mate]
            rc(four, four, ss.at[9], rs.at[9, h], d_core).start()

        return carry

    lax.fori_loop(0, HEADS_DEV + 3, round_, 0)

    for n in (0, 1, 2, 7):
        sent(wbuf.at[:, 0, 0], ss.at[n])
    sent(wbuf.at[:, 0, 0, 0:FAR], ss.at[3])
    sent(wbuf.at[:, 0, 0, FAR:WID], ss.at[4])
    for n in (5, 6):
        sent(wbuf.at[:, 0, 0, 0:VIA], ss.at[n])
    for n in (12, 13):
        sent(wbuf.at[:, 0, 0, VIA:WID], ss.at[n])
    for n in (8, 9):
        sent(wbuf.at[:, 0], ss.at[n])

    @pl.when(tok < 15)
    def _():
        sent(kvwin.at[:, 0:TOK], ss.at[11])

    sent(stage.at[0:7], nss.at[0])
    for n in range(1, 6):
        sent(nbuf.at[0:2, :, mine], nss.at[n])
    for n in range(6, 10):
        sent(nbuf.at[0, :, mine], nss.at[n])

    @pl.when(b_src == k)
    def _():
        sent(w_ref.at[0], ass.at[0])

    sent(abuf.at[0], ass.at[1])
    for s in range(3):
        sent(dpart.at[s], dss.at[s])

    @pl.when(lane0)
    def _():
        sent(ubuf, uss)

    @pl.when(lane1)
    def _():
        sent(wbuf.at[:, 0, 0], ss.at[10])
        sent(out_att, oss.at[0])
        sent(out_k, oss.at[1])
        sent(out_v, oss.at[2])

    got(out_att, os_.at[0])
    got(out_k, os_.at[1])
    got(out_v, os_.at[2])


def run_fused(*operands):
    bf, f32, i32 = jnp.bfloat16, jnp.float32, jnp.int32
    dma = pltpu.SemaphoreType.DMA
    any_ = pl.BlockSpec(memory_space=pl.ANY)
    vmem = pl.BlockSpec(memory_space=pltpu.VMEM)
    wide = HEADS_DEV * HEAD_DIM
    return pl.pallas_call(
        fused,
        out_shape=(
            jax.ShapeDtypeStruct((TOK, wide), bf),
            jax.ShapeDtypeStruct((KEEP, wide), bf),
            jax.ShapeDtypeStruct((KEEP, wide), bf),
            jax.ShapeDtypeStruct((SLOTS, 128), i32),
        ),
        in_specs=[any_] * 4 + [vmem] * 4,
        out_specs=(any_, any_, any_, vmem),
        scratch_shapes=[
            pltpu.VMEM((HEADS_DEV, 4, 4, WID, 3 * HEAD_DIM), bf),
            pltpu.VMEM((4, 4, TOK, WID), bf),
            pltpu.VMEM((2, 4, 8, 16 * WID), bf),
            pltpu.VMEM((SLOTS, 2, RANK, wide), bf),
            pltpu.VMEM((8, WID, QUARTER), bf),
            pltpu.VMEM((8, QUARTER, WID), bf),
            pltpu.VMEM((HEADS_DEV, 2 * TOK, 2 * HEAD_DIM), bf),
            pltpu.VMEM((TOK, HEAD_DIM), bf),
            pltpu.VMEM((HEADS_DEV, TOK, HEAD_DIM), bf),
            pltpu.VMEM((TOK, 3 * HEAD_DIM), f32),
            pltpu.VMEM((4, TOK, 2 * RANK), bf),
            pltpu.VMEM((3, TOK, 2 * RANK), bf),
            pltpu.VMEM((TOK, 2 * SLOTS * RANK), bf),
            pltpu.VMEM((TOK, 1), i32),
            pltpu.VMEM((TOK, 1), i32),
            dma((14, HEADS_DEV)),
            dma((14,)),
            dma((10,)),
            dma((10,)),
            dma((2,)),
            dma((2,)),
            dma((3,)),
            dma((3,)),
            dma,
            dma,
            dma((8,)),
            dma((3,)),
            dma((3,)),
        ],
        compiler_params=pltpu.CompilerParams(
            collective_id=0, has_side_effects=True, vmem_limit_bytes=67_043_328
        ),
    )(*operands)


def assemble(page_ref, k_ref, v_ref, out_ref):
    for i in range(PER_STEP):
        one_page(pl.program_id(0) * PER_STEP + i, i, page_ref, k_ref, v_ref, out_ref)


def one_page(s, i, page_ref, k_ref, v_ref, out_ref):
    offset, used = page_ref[s, 0], page_ref[s, 1]
    span = PAGE + 16
    first = jnp.minimum(offset // 16 * 16, KEEP - span)
    first = pl.multiple_of(first, 16)
    lines = jnp.concatenate([k_ref[pl.ds(first, span), :], v_ref[pl.ds(first, span), :]], axis=0)
    n = lax.broadcasted_iota(jnp.int32, (2 * PAGE, 2 * span), 0)
    m = lax.broadcasted_iota(jnp.int32, (2 * PAGE, 2 * span), 1)
    pick = (m == (n % 2) * span + n // 2 + (offset - first)) & (n // 2 < used)
    rows = jnp.dot(pick.astype(jnp.bfloat16), lines, preferred_element_type=jnp.float32)
    out_ref[i] = rows.astype(jnp.bfloat16).reshape(PAGE, 2, lines.shape[1])


def run_assemble(page, keys, values):
    wide = keys.shape[1]
    vmem = pl.BlockSpec(memory_space=pltpu.VMEM)
    return pl.pallas_call(
        assemble,
        grid=(SLOTS_DEV // PER_STEP,),
        out_shape=jax.ShapeDtypeStruct((SLOTS_DEV, PAGE, 2, wide), keys.dtype),
        in_specs=[pl.BlockSpec(memory_space=pltpu.SMEM), vmem, vmem],
        out_specs=pl.BlockSpec((PER_STEP, PAGE, 2, wide), lambda s: (s, 0, 0, 0)),
    )(page, keys, values)


def local(
    normed,
    projection_weight,
    adapter_down_weight,
    adapter_up_weight,
    packed_prompt_length,
    prompt_adapter_ids,
    slot_adapter_ids,
    prompt_page_slots,
):
    attended, keys, values, page = run_fused(
        normed.T,
        jnp.transpose(projection_weight, (1, 0, 2)),
        jnp.transpose(adapter_down_weight, (1, 2, 0))[0],
        adapter_up_weight,
        packed_prompt_length[None, :],
        prompt_adapter_ids[None, :],
        slot_adapter_ids[None, :],
        prompt_page_slots.T,
    )
    return attended, run_assemble(page, keys, values)


def solution(mesh):
    placed = (
        P(None, "col"),
        P("col", None, "row"),
        P(None, "col", None),
        P(None, None, None, "row"),
        P(),
        P(),
        P(),
        P(),
    )
    return jax.shard_map(
        local,
        mesh=mesh,
        in_specs=placed,
        out_specs=(P("col", "row"), P("col", None, None, "row")),
        check_vma=False,
    )
```

```python
import jax
import jax.numpy as jnp
from jax import lax
from jax.experimental import pallas as pl
from jax.experimental.pallas import tpu as pltpu
from jax.sharding import PartitionSpec as P

HEAD_DIM = 128
PAGE = 128
SLOTS_DEV = 10
PER_STEP = 2
HEADS_DEV = 7
KV_BLOCKS = 14
SLOTS = 16
RANK = 16
TOK = 512
WID = 448
KEEP = 640
BAND = 640
PROMPTS = 64
QUARTER = 128
FAR = 224
VIA = 432

adapter_scale = 2.0
masked_score = -1e30
MESH = pl.DeviceIdType.MESH


def place():
    col = lax.axis_index("col")
    row = lax.axis_index("row")
    x, y = col // 4, col % 4
    z, k = row // 2, row % 2
    p = y // 2
    d = (k + p) % 2
    tok = x * 4 + y + d * (3 - 2 * y)
    return x, y, z, k, p, d, tok


def dev(x, y, z, k):
    return (z * 2 + k, x * 4 + y)


def holder(t, z, p):
    x, y = t // 4, t % 4
    e = (y // 2 + p) % 2
    return dev(x, y + e * (3 - 2 * y), z, (p + e) % 2)


def to_column(line, n):
    r = lax.broadcasted_iota(jnp.int32, (n, n), 0)
    c = lax.broadcasted_iota(jnp.int32, (n, n), 1)
    return jnp.sum(jnp.where(r == c, line, 0.0), axis=1, keepdims=True)


def fused(
    nt_ref,
    w_ref,
    at_ref,
    up_ref,
    len_ref,
    ask_ref,
    slot_ref,
    page_ref,
    out_att,
    out_k,
    out_v,
    out_page,
    wbuf,
    nbuf,
    abuf,
    ubuf,
    raw,
    stage,
    kvwin,
    qbuf,
    att,
    acc,
    dpart,
    drecv,
    spread,
    tslot,
    low,
    rs,
    ss,
    ns,
    nss,
    as_,
    ass,
    ds_,
    dss,
    us,
    uss,
    raws,
    os_,
    oss,
):
    x, y, z, k, p, d, tok = place()
    xp, xm, xf = (x + 1) % 4, (x + 3) % 4, (x + 2) % 4
    zp, zm, zf = (z + 1) % 4, (z + 3) % 4, (z + 2) % 4
    mate = y + 1 - 2 * (y % 2)
    d_xp = dev(xp, y, z, k)
    d_xm = dev(xm, y, z, k)
    d_m = dev(x, mate, z, k)
    d_core = dev(x, y, z, 1 - k)
    d_swap = dev(x, 3 - y, z, 1 - k)
    d_cross = dev(x, 3 - y, z, k)
    d_zp = dev(x, y, zp, k)
    d_zm = dev(x, y, zm, k)
    b_own = (y + d) % 2
    q_own = 2 * d + b_own
    q_mate = 2 * d + 1 - b_own
    o_own = 2 * (1 - d) + (y + 1 - d) % 2
    o_mate = 2 * (1 - d) + 1 - (y + 1 - d) % 2
    lane0 = d == 0
    lane1 = d == 1
    b_src = y % 2

    def rc(src, dst, send, recv, to):
        return pltpu.make_async_remote_copy(
            src_ref=src, dst_ref=dst, send_sem=send, recv_sem=recv, device_id=to, device_id_type=MESH
        )

    def got(ref, sem):
        rc(ref, ref, ss.at[0], sem, d_core).wait_recv()

    def sent(ref, sem):
        rc(ref, ref, sem, rs.at[0, 0], d_core).wait_send()

    barrier = pltpu.get_barrier_semaphore()

    def greet(to):
        pl.semaphore_signal(barrier, inc=1, device_id=to, device_id_type=MESH)

    near = [d_core, d_swap, d_cross, d_zp, d_zm, d_m]
    for xt in (xp, xm, xf):
        near += [dev(xt, y, z, k), dev(xt, mate, z, k)]
    for to in near:
        greet(to)

    greet(holder((tok + 1) % 16, z, p))
    greet(holder((tok + 15) % 16, z, p))
    def w_own(h, kind_of_lane=None):
        for j in range(3):
            g = 3 * h + j
            late = g // KV_BLOCKS
            kind = (1 + g % 2) * (1 - late)
            head = late * (g - KV_BLOCKS) + (1 - late) * (g // 2)
            src = w_ref.at[kind, :, pl.ds(pl.multiple_of(head * HEAD_DIM, HEAD_DIM), HEAD_DIM)]
            lanes = pl.ds(j * HEAD_DIM, HEAD_DIM)

            if kind_of_lane in (None, 0):

                @pl.when(lane0)
                def _():
                    pltpu.make_async_copy(src, wbuf.at[h, q_own, x, :, lanes], rs.at[10, h]).start()

            if kind_of_lane in (None, 1):

                @pl.when(lane1)
                def _():
                    rc(src, wbuf.at[h, 2 + b_src, x, :, lanes], ss.at[10], rs.at[10, h], d_swap).start()

    def w_first(h):
        own = wbuf.at[h, q_own, x]
        got(own, rs.at[10, h])
        rc(own, own, ss.at[0], rs.at[0, h], d_xp).start()
        rc(own, own, ss.at[1], rs.at[1, h], d_xm).start()
        rc(own, own, ss.at[2], rs.at[2, h], d_m).start()

    def block_of(n):
        xt = n // 2
        yt = y + (n % 2) * (mate - y)
        tt = xt * 4 + yt + d * (3 - 2 * yt)
        first = pl.multiple_of(tt * TOK + z * QUARTER, QUARTER)
        return xt, yt, first

    def loading(n):
        columns = pl.ds(block_of(n)[2], QUARTER)
        return pltpu.make_async_copy(nt_ref.at[:, columns], raw.at[n], raws.at[n])

    def load(n, c):
        loading(n).start()
        return c

    lax.fori_loop(0, 8, load, 0)
    for h in range(3):
        w_own(h, 0)
    mine = pl.ds(pl.multiple_of(z * QUARTER, QUARTER), QUARTER)
    ranks = pl.ds(pl.multiple_of(z * 8, 8), 8)

    def turn(n, c):
        loading(n).wait()
        stage[n] = raw[n].T
        return c

    lax.fori_loop(0, 8, turn, 0)

    @pl.when(tok == 0)
    def _():
        kvwin[:, 0:TOK, :] = jnp.zeros((HEADS_DEV, TOK, 2 * HEAD_DIM), jnp.bfloat16)

    f32 = jnp.float32
    lens = len_ref[...].astype(f32)
    r64 = lax.broadcasted_iota(jnp.int32, (PROMPTS, PROMPTS), 0)
    c64 = lax.broadcasted_iota(jnp.int32, (PROMPTS, PROMPTS), 1)
    starts = jnp.sum(jnp.where(r64 < c64, to_column(lens, PROMPTS), 0.0), axis=0, keepdims=True)
    slot_col = to_column(slot_ref[...].astype(f32), SLOTS)
    s_row = lax.broadcasted_iota(jnp.int32, (SLOTS, PROMPTS), 0)
    slot_of = jnp.sum(
        jnp.where(slot_col == ask_ref[...].astype(f32), s_row.astype(f32), 0.0), axis=0, keepdims=True
    )
    at = (lax.broadcasted_iota(jnp.int32, (TOK, PROMPTS), 0) + tok * TOK).astype(f32)
    inside = (at >= starts) & (at < starts + lens)
    tslot[...] = jnp.sum(jnp.where(inside, slot_of, 0.0), axis=1, keepdims=True).astype(jnp.int32)
    first = jnp.sum(jnp.where(inside, starts, 0.0), axis=1, keepdims=True).astype(jnp.int32)
    low[...] = first - (tok - 1) * TOK
    my_col = x * 4 + y
    where_ = s_row + my_col * SLOTS_DEV
    offset = jnp.zeros((SLOTS, 1), f32)
    used = jnp.zeros((SLOTS, 1), f32)
    for j in range(page_ref.shape[0]):
        hit = page_ref[j : j + 1, :] == where_
        offset += jnp.sum(jnp.where(hit, starts + float(PAGE * j), 0.0), axis=1, keepdims=True)
        used += jnp.sum(
            jnp.where(hit, jnp.clip(lens - float(PAGE * j), 0.0, float(PAGE)), 0.0), axis=1, keepdims=True
        )
    base = my_col * TOK + TOK - KEEP
    offset = jnp.clip(offset.astype(jnp.int32) - base, 0, KEEP - 1)
    lane = lax.broadcasted_iota(jnp.int32, (SLOTS, 128), 1)
    out_page[...] = jnp.where(lane == 0, offset, used.astype(jnp.int32))

    pl.semaphore_wait(barrier, len(near) + 2)
    for h in range(3):
        w_own(h, 1)

    def scatter(n, c):
        xt, yt, _ = block_of(n)
        itself = (xt == x) & (n % 2 == 0)

        @pl.when(itself)
        def _():
            pltpu.make_async_copy(stage.at[n], nbuf.at[b_src, x, mine], ns.at[0]).start()

        @pl.when(jnp.logical_not(itself))
        def _():
            rc(stage.at[n], nbuf.at[b_src, x, mine], nss.at[0], ns.at[0], dev(xt, yt, z, k)).start()

        return c

    @pl.when(lane0)
    def _():
        w_first(0)

    lax.fori_loop(0, 8, scatter, 0)

    @pl.when(lane1)
    def _():
        w_first(0)

    def maps(n, c):
        xt, yt, _ = block_of(n)
        itself = (xt == x) & (n % 2 == 0)

        @pl.when((b_src == k) & itself)
        def _():
            pltpu.make_async_copy(at_ref.at[ranks], abuf.at[b_src, x], as_.at[0]).start()

        @pl.when((b_src == k) & jnp.logical_not(itself))
        def _():
            rc(at_ref.at[ranks], abuf.at[b_src, x], ass.at[0], as_.at[0], dev(xt, yt, z, k)).start()

        return c

    lax.fori_loop(0, 8, maps, 0)

    @pl.when(lane0)
    def _():
        pltpu.make_async_copy(up_ref, ubuf, us).start()
        rc(up_ref, ubuf, uss, us, d_core).start()

    def down():
        total = jnp.zeros((TOK, 64), f32)
        for q in range(4):
            for xx in range(4):
                begin = (xx * 2 + (p + q // 2) % 2) * (2 * WID)
                pair = abuf[:, :, :, pl.ds(pl.multiple_of(begin, HEAD_DIM), 2 * WID)].reshape(64, 2 * WID)
                part = pair[:, (q % 2) * WID : (q % 2 + 1) * WID]
                total = total + lax.dot_general(
                    nbuf[q, xx], part, (((1,), (1,)), ((), ())), preferred_element_type=f32
                )
        n = lax.broadcasted_iota(jnp.int32, (TOK, 64), 1)
        slot = ((n // 8) % 4) * 4 + 2 * p + n // 32
        term = jnp.where(slot == tslot[...], total, 0.0).astype(jnp.bfloat16)
        rows = lax.broadcasted_iota(jnp.int32, (64, 2 * RANK), 0)
        cols = lax.broadcasted_iota(jnp.int32, (64, 2 * RANK), 1)
        fold = (cols == rows % 8 + 8 * z).astype(jnp.bfloat16)
        dpart[0] = jnp.dot(term, fold, preferred_element_type=f32).astype(jnp.bfloat16)
        z1 = z + 1 - 2 * (z % 2)
        for s, to in enumerate((d_cross, dev(x, y, z1, k), dev(x, y, 3 - z, k))):
            rc(dpart.at[s], drecv.at[s], dss.at[s], ds_.at[s], to).start()
            if s < 2:
                mm(0, s)
            got(drecv.at[s], ds_.at[s])
            dpart[s + 1] = dpart[s] + drecv[s]
        rows = lax.broadcasted_iota(jnp.int32, (2 * RANK, 2 * SLOTS * RANK), 0)
        cols = lax.broadcasted_iota(jnp.int32, (2 * RANK, 2 * SLOTS * RANK), 1)
        place_of = (rows == cols % RANK + RANK * (cols // (SLOTS * RANK))).astype(jnp.bfloat16)
        wide = jnp.dot(dpart[3], place_of, preferred_element_type=f32)
        slot_at = (lax.broadcasted_iota(jnp.int32, (TOK, 2 * SLOTS * RANK), 1) // RANK) % SLOTS
        spread[...] = jnp.where(slot_at == tslot[...], wide, 0.0).astype(jnp.bfloat16)
        got(ubuf, us)
        finish(0)

    def head_lanes(h):
        return pl.ds(pl.multiple_of(h * HEAD_DIM, HEAD_DIM), HEAD_DIM)

    def deliver(moves):
        for src, dst, n in moves:

            @pl.when(lane0)
            def _():
                pltpu.make_async_copy(src, dst, os_.at[n]).start()

            @pl.when(lane1)
            def _():
                rc(src, dst, oss.at[n], os_.at[n], d_swap).start()

    def mm(h, n):
        def part(q):
            s = jnp.dot(nbuf[q, 0], wbuf[h, q, 0], preferred_element_type=f32)
            for xx in range(1, 4):
                s = s + jnp.dot(nbuf[q, xx], wbuf[h, q, xx], preferred_element_type=f32)
            acc[...] += s

        def theirs(own):
            return own * o_own + (1 - own) * o_mate

        @pl.when(n == 0)
        def _():
            acc[...] = jnp.zeros_like(acc)

        part((1 - n) * q_own + n * q_mate)
        got(wbuf.at[h, theirs(1 - n)], rs.at[8 + n, h])
        part(theirs(1 - n))

    def qkv(h, n):
        mm(h, n)

        @pl.when(n == 1)
        def _():
            finish(h)

    def finish(r):
        half = SLOTS * RANK

        def one(j, carry):
            g = 3 * r + j
            block = acc.at[:, head_lanes(j)]

            @pl.when((g < KV_BLOCKS) & (g % 2 == 0))
            def _():
                kvwin[g // 2, TOK:, :HEAD_DIM] = block[...].astype(jnp.bfloat16)

            @pl.when((g < KV_BLOCKS) & (g % 2 == 1))
            def _():
                h = g // 2
                up_v = ubuf[:, 1, :, head_lanes(h)].reshape(half, HEAD_DIM)
                dv = jnp.dot(spread[:, half:], up_v, preferred_element_type=f32)
                kvwin[h, TOK:, HEAD_DIM:] = (block[...] + adapter_scale * dv).astype(jnp.bfloat16)

                @pl.when(tok < 15)
                def _():
                    mine_ = kvwin.at[h, TOK:]
                    theirs_ = kvwin.at[h, 0:TOK]
                    rc(mine_, theirs_, ss.at[11], rs.at[11, h], holder(tok + 1, z, p)).start()

                deliver(
                    (
                        (kvwin.at[h, TOK:, 0:HEAD_DIM], out_k.at[KEEP - TOK :, head_lanes(h)], 1),
                        (kvwin.at[h, TOK:, HEAD_DIM:], out_v.at[KEEP - TOK :, head_lanes(h)], 2),
                    )
                )

            @pl.when(g >= KV_BLOCKS)
            def _():
                h = g - KV_BLOCKS
                up_q = ubuf[:, 0, :, head_lanes(h)].reshape(half, HEAD_DIM)
                dq = jnp.dot(spread[:, :half], up_q, preferred_element_type=f32)
                qbuf[...] = (block[...] + adapter_scale * dq).astype(jnp.bfloat16)
                attend(h)

            return carry

        lax.fori_loop(0, 3, one, 0)

    def attend(h):
        @pl.when(tok > 0)
        def _():
            got(kvwin.at[h, 0:TOK], rs.at[11, h])

        early = pl.ds(2 * TOK - KEEP, KEEP - TOK)
        deliver(
            (
                (kvwin.at[h, early, 0:HEAD_DIM], out_k.at[0 : KEEP - TOK, head_lanes(h)], 1),
                (kvwin.at[h, early, HEAD_DIM:], out_v.at[0 : KEEP - TOK, head_lanes(h)], 2),
            )
        )
        for i in range(4):
            r0 = i * 128
            qi = qbuf[r0 : r0 + 128, :]
            ki = kvwin[h, r0 : r0 + BAND, :HEAD_DIM]
            vi = kvwin[h, r0 : r0 + BAND, HEAD_DIM:]
            s = lax.dot_general(qi, ki, (((1,), (1,)), ((), ())), preferred_element_type=f32)
            s = s * (HEAD_DIM**-0.5)
            u = lax.broadcasted_iota(jnp.int32, (128, BAND), 1)
            r = lax.broadcasted_iota(jnp.int32, (128, BAND), 0)
            lo = low[r0 : r0 + 128, :] - r0
            s = jnp.where((u >= lo) & (u <= r + TOK), s, masked_score)
            e = jnp.exp(s - jnp.max(s, axis=1, keepdims=True))
            total = jnp.sum(e, axis=1, keepdims=True)
            o = jnp.dot(e.astype(jnp.bfloat16), vi, preferred_element_type=f32)
            att[h, r0 : r0 + 128, :] = (o / total).astype(jnp.bfloat16)

        deliver(((att.at[h], out_att.at[:, head_lanes(h)], 0),))

    def tokens_of(zz):
        return pl.ds(pl.multiple_of(zz * QUARTER, QUARTER), QUARTER)

    def round_(i, carry):
        @pl.when(i + 3 < HEADS_DEV)
        def _():
            w_own(i + 3)

        @pl.when(i + 1 < HEADS_DEV)
        def _():
            w_first(i + 1)

        @pl.when(i < HEADS_DEV)
        def _():
            h = i
            got(wbuf.at[h, q_own, xm], rs.at[0, h])
            lower = wbuf.at[h, q_own, xm, 0:FAR]
            rc(lower, lower, ss.at[3], rs.at[3, h], d_xp).start()
            rest = wbuf.at[h, q_own, xm, VIA:WID]
            rc(rest, rest, ss.at[12], rs.at[12, h], d_m).start()
            got(wbuf.at[h, q_own, xp], rs.at[1, h])
            upper = wbuf.at[h, q_own, xp, FAR:WID]
            rc(upper, upper, ss.at[4], rs.at[4, h], d_xm).start()
            rest = wbuf.at[h, q_own, xp, VIA:WID]
            rc(rest, rest, ss.at[13], rs.at[13, h], d_m).start()
            got(wbuf.at[h, q_mate, x], rs.at[2, h])
            other = wbuf.at[h, q_mate, x, 0:VIA]
            rc(other, other, ss.at[5], rs.at[5, h], d_xp).start()
            rc(other, other, ss.at[6], rs.at[6, h], d_xm).start()

        @pl.when((i >= 1) & (i < HEADS_DEV + 1))
        def _():
            h = i - 1
            got(wbuf.at[h, q_own, xf, 0:FAR], rs.at[3, h])
            got(wbuf.at[h, q_own, xf, FAR:WID], rs.at[4, h])
            far = wbuf.at[h, q_own, xf]
            rc(far, far, ss.at[7], rs.at[7, h], d_m).start()
            four = wbuf.at[h, q_own]
            rc(four, four, ss.at[8], rs.at[8, h], d_core).start()

        @pl.when(i == 0)
        def _():
            got(nbuf.at[0:2, :, mine], ns.at[0])
            u = nbuf.at[0:2, :, mine]
            rc(u, nbuf.at[2:4, :, mine], nss.at[1], ns.at[1], d_cross).start()
            rc(u, u, nss.at[2], ns.at[2], d_zp).start()
            rc(u, u, nss.at[3], ns.at[3], d_zm).start()

        @pl.when(i == 1)
        def _():
            u = nbuf.at[2:4, :, mine]
            got(abuf.at[k], as_.at[0])
            rc(abuf.at[k], abuf.at[k], ass.at[1], as_.at[1], d_core).start()
            got(u, ns.at[1])
            rc(u, u, nss.at[4], ns.at[4], d_zp).start()
            rc(u, u, nss.at[5], ns.at[5], d_zm).start()
            got(nbuf.at[0:2, :, tokens_of(zm)], ns.at[2])
            u = nbuf.at[0, :, tokens_of(zm)]
            rc(u, u, nss.at[6], ns.at[6], d_zp).start()
            got(nbuf.at[0:2, :, tokens_of(zp)], ns.at[3])
            u = nbuf.at[1, :, tokens_of(zp)]
            rc(u, u, nss.at[7], ns.at[7], d_zm).start()

        @pl.when(i == 2)
        def _():
            got(nbuf.at[2:4, :, tokens_of(zm)], ns.at[4])
            u = nbuf.at[2, :, tokens_of(zm)]
            rc(u, u, nss.at[8], ns.at[8], d_zp).start()
            got(nbuf.at[2:4, :, tokens_of(zp)], ns.at[5])
            u = nbuf.at[3, :, tokens_of(zp)]
            rc(u, u, nss.at[9], ns.at[9], d_zm).start()

        @pl.when(i == 4)
        def _():
            for q in range(4):
                got(nbuf.at[q, :, tokens_of(zf)], ns.at[6 + q])
            got(abuf.at[1 - k], as_.at[1])
            down()

        def first_step(i):
            return 2 * i - 5 - 4 // i

        @pl.when((i >= 4) & (i < HEADS_DEV + 3))
        def _():
            def one(step, c):
                @pl.when(step < 2 * HEADS_DEV)
                def _():
                    qkv(step // 2, step % 2)

                return c

            lax.fori_loop(first_step(i), first_step(i + 1), one, 0)

        @pl.when((i >= 2) & (i < HEADS_DEV + 2))
        def _():
            h = i - 2
            got(wbuf.at[h, q_mate, xm, 0:VIA], rs.at[5, h])
            got(wbuf.at[h, q_mate, xp, 0:VIA], rs.at[6, h])
            got(wbuf.at[h, q_mate, xm, VIA:WID], rs.at[12, h])
            got(wbuf.at[h, q_mate, xp, VIA:WID], rs.at[13, h])
            got(wbuf.at[h, q_mate, xf], rs.at[7, h])
            four = wbuf.at[h, q_mate]
            rc(four, four, ss.at[9], rs.at[9, h], d_core).start()

        return carry

    lax.fori_loop(0, HEADS_DEV + 3, round_, 0)

    for n in (0, 1, 2, 7):
        sent(wbuf.at[:, 0, 0], ss.at[n])
    sent(wbuf.at[:, 0, 0, 0:FAR], ss.at[3])
    sent(wbuf.at[:, 0, 0, FAR:WID], ss.at[4])
    for n in (5, 6):
        sent(wbuf.at[:, 0, 0, 0:VIA], ss.at[n])
    for n in (12, 13):
        sent(wbuf.at[:, 0, 0, VIA:WID], ss.at[n])
    for n in (8, 9):
        sent(wbuf.at[:, 0], ss.at[n])

    @pl.when(tok < 15)
    def _():
        sent(kvwin.at[:, 0:TOK], ss.at[11])

    sent(stage.at[0:7], nss.at[0])
    for n in range(1, 6):
        sent(nbuf.at[0:2, :, mine], nss.at[n])
    for n in range(6, 10):
        sent(nbuf.at[0, :, mine], nss.at[n])

    @pl.when(b_src == k)
    def _():
        sent(w_ref.at[0], ass.at[0])

    sent(abuf.at[0], ass.at[1])
    for s in range(3):
        sent(dpart.at[s], dss.at[s])

    @pl.when(lane0)
    def _():
        sent(ubuf, uss)

    @pl.when(lane1)
    def _():
        sent(wbuf.at[:, 0, 0], ss.at[10])
        sent(out_att, oss.at[0])
        sent(out_k, oss.at[1])
        sent(out_v, oss.at[2])

    got(out_att, os_.at[0])
    got(out_k, os_.at[1])
    got(out_v, os_.at[2])


def run_fused(*operands):
    bf, f32, i32 = jnp.bfloat16, jnp.float32, jnp.int32
    dma = pltpu.SemaphoreType.DMA
    any_ = pl.BlockSpec(memory_space=pl.ANY)
    vmem = pl.BlockSpec(memory_space=pltpu.VMEM)
    wide = HEADS_DEV * HEAD_DIM
    return pl.pallas_call(
        fused,
        out_shape=(
            jax.ShapeDtypeStruct((TOK, wide), bf),
            jax.ShapeDtypeStruct((KEEP, wide), bf),
            jax.ShapeDtypeStruct((KEEP, wide), bf),
            jax.ShapeDtypeStruct((SLOTS, 128), i32),
        ),
        in_specs=[any_] * 4 + [vmem] * 4,
        out_specs=(any_, any_, any_, vmem),
        scratch_shapes=[
            pltpu.VMEM((HEADS_DEV, 4, 4, WID, 3 * HEAD_DIM), bf),
            pltpu.VMEM((4, 4, TOK, WID), bf),
            pltpu.VMEM((2, 4, 8, 16 * WID), bf),
            pltpu.VMEM((SLOTS, 2, RANK, wide), bf),
            pltpu.VMEM((8, WID, QUARTER), bf),
            pltpu.VMEM((8, QUARTER, WID), bf),
            pltpu.VMEM((HEADS_DEV, 2 * TOK, 2 * HEAD_DIM), bf),
            pltpu.VMEM((TOK, HEAD_DIM), bf),
            pltpu.VMEM((HEADS_DEV, TOK, HEAD_DIM), bf),
            pltpu.VMEM((TOK, 3 * HEAD_DIM), f32),
            pltpu.VMEM((4, TOK, 2 * RANK), bf),
            pltpu.VMEM((3, TOK, 2 * RANK), bf),
            pltpu.VMEM((TOK, 2 * SLOTS * RANK), bf),
            pltpu.VMEM((TOK, 1), i32),
            pltpu.VMEM((TOK, 1), i32),
            dma((14, HEADS_DEV)),
            dma((14,)),
            dma((10,)),
            dma((10,)),
            dma((2,)),
            dma((2,)),
            dma((3,)),
            dma((3,)),
            dma,
            dma,
            dma((8,)),
            dma((3,)),
            dma((3,)),
        ],
        compiler_params=pltpu.CompilerParams(
            collective_id=0, has_side_effects=True, vmem_limit_bytes=67_043_328
        ),
    )(*operands)


def assemble(page_ref, k_ref, v_ref, out_ref):
    for i in range(PER_STEP):
        one_page(pl.program_id(0) * PER_STEP + i, i, page_ref, k_ref, v_ref, out_ref)


def one_page(s, i, page_ref, k_ref, v_ref, out_ref):
    offset, used = page_ref[s, 0], page_ref[s, 1]
    span = PAGE + 16
    first = jnp.minimum(offset // 16 * 16, KEEP - span)
    first = pl.multiple_of(first, 16)
    lines = jnp.concatenate([k_ref[pl.ds(first, span), :], v_ref[pl.ds(first, span), :]], axis=0)
    n = lax.broadcasted_iota(jnp.int32, (2 * PAGE, 2 * span), 0)
    m = lax.broadcasted_iota(jnp.int32, (2 * PAGE, 2 * span), 1)
    pick = (m == (n % 2) * span + n // 2 + (offset - first)) & (n // 2 < used)
    rows = jnp.dot(pick.astype(jnp.bfloat16), lines, preferred_element_type=jnp.float32)
    out_ref[i] = rows.astype(jnp.bfloat16).reshape(PAGE, 2, lines.shape[1])


def run_assemble(page, keys, values):
    wide = keys.shape[1]
    vmem = pl.BlockSpec(memory_space=pltpu.VMEM)
    return pl.pallas_call(
        assemble,
        grid=(SLOTS_DEV // PER_STEP,),
        out_shape=jax.ShapeDtypeStruct((SLOTS_DEV, PAGE, 2, wide), keys.dtype),
        in_specs=[pl.BlockSpec(memory_space=pltpu.SMEM), vmem, vmem],
        out_specs=pl.BlockSpec((PER_STEP, PAGE, 2, wide), lambda s: (s, 0, 0, 0)),
    )(page, keys, values)


def local(
    normed,
    projection_weight,
    adapter_down_weight,
    adapter_up_weight,
    packed_prompt_length,
    prompt_adapter_ids,
    slot_adapter_ids,
    prompt_page_slots,
):
    attended, keys, values, page = run_fused(
        normed.T,
        jnp.transpose(projection_weight, (1, 0, 2)),
        jnp.transpose(adapter_down_weight, (1, 2, 0))[0],
        adapter_up_weight,
        packed_prompt_length[None, :],
        prompt_adapter_ids[None, :],
        slot_adapter_ids[None, :],
        prompt_page_slots.T,
    )
    return attended, run_assemble(page, keys, values)


def solution(mesh):
    placed = (
        P(None, "col"),
        P("col", None, "row"),
        P(None, "col", None),
        P(None, None, None, "row"),
        P(),
        P(),
        P(),
        P(),
    )
    return jax.shard_map(
        local,
        mesh=mesh,
        in_specs=placed,
        out_specs=(P("col", "row"), P("col", None, None, "row")),
        check_vma=False,
    )
```
